32 devices in a mesh: row: 8 (over y, x, core), col: 4 (over z).
Axes of the slice: x: 2, y: 2, z: 4, core: 2. Of those that a mesh axis runs over, the one named last changes fastest.
Arguments:
- teacher: bfloat16 [37, 1024, 1024], P(None, 'row', 'col'), may hold values from -320 to 320
- features: bfloat16 [64, 1024, 1024], P(None, 'row', 'col'), may hold values from -6 to 6
- valid: int32 [1024], replicated, may hold values from 0 to 1
- w_conv: bfloat16 [64, 64, 3, 3], replicated, may hold values from -0.25 to 0.25
- b_conv: float32 [64], replicated, may hold values from -3 to 3
- w_head: bfloat16 [37, 64], replicated, may hold values from -42 to 42
- b_head: float32 [37], replicated, may hold values from -4 to 4
Outputs:
- pair_loss: float32 [1024, 1024], P('row', 'col')
- loss: float32 [], replicated
- grad_conv: float32 [64, 64, 3, 3], replicated
- grad_conv_bias: float32 [64], replicated
- grad_head: float32 [37, 64], replicated
- grad_head_bias: float32 [37], replicated
The draws below stay inside these ranges and needn't reach their ends.
All inputs are finite; a program needn't handle non-finite values.
Results may differ from the reference program's by a relative error of at most 0.004.
Values may be sent and summed in bfloat16 or wider, within the bound.
A program may use at most 192 MiB of HBM per device.

```python
import jax
import jax.numpy as jnp
from jax import lax

CH = 64
BINS = 37
DILATION_STEP = 4
RESIDUE_ROWS = 128
NRES = 1024
N_ROW = 8


def draw_teacher(key, part):
    base = jnp.clip(jax.random.normal(key, (BINS, NRES, NRES), jnp.float32), -6.0, 6.0) * 3.0
    return base.astype(jnp.bfloat16)


def draw_valid(key, part):
    places = jnp.arange(NRES, dtype=jnp.int32)
    rolls = jax.random.randint(key, (NRES,), 0, 1000, dtype=jnp.int32)
    limits = 250 + 700 * places // NRES
    marks = (rolls < limits).astype(jnp.int32)
    return marks.at[0].set(1)


def draw_w_head(key, part):
    base = jnp.clip(jax.random.normal(key, (BINS, CH), jnp.float32), -4.0, 4.0) * CH ** (-0.5)
    return base.astype(jnp.bfloat16)


def block_levels(key, shape, cuts, low, high):
    gain, own = 1.0, jax.random.fold_in(key, 6)
    for position, parts in cuts:
        draws = jnp.exp(jax.random.uniform(jax.random.fold_in(own, position), (parts,), jnp.float32, low / len(cuts), high / len(cuts)))
        gain = gain * jnp.repeat(draws, shape[position] // parts).reshape([-1 if axis == position else 1 for axis in range(len(shape))])
    return gain


def normal_values(stream_key, dims, width, bound, cuts=(), held_as=jnp.bfloat16):
    array = width * jax.random.normal(stream_key, dims, jnp.float32)
    if cuts:
        array = array * block_levels(stream_key, dims, cuts, -0.22, 0.18)
    return jnp.clip(array, -bound, bound).astype(held_as)


def setup_inputs(seed: int = 0) -> dict:
    keys = jax.random.split(jax.random.key(seed), 8)
    teacher = draw_teacher(jax.random.fold_in(keys[7], 71), 0)
    features = normal_values(keys[1], (CH, NRES, NRES), 1.0, 6.0, ((1, 8), (2, 4)))
    valid = draw_valid(jax.random.fold_in(keys[7], 71), 0)
    w_conv = normal_values(keys[3], (CH, CH, 3, 3), (CH * 9) ** -0.5, 0.25)
    b_conv = normal_values(keys[4], (CH,), 0.5, 3.0, (), jnp.float32)
    w_head = draw_w_head(jax.random.fold_in(keys[7], 71), 0)
    b_head = normal_values(keys[6], (BINS,), 1.0, 4.0, (), jnp.float32)
    return {"teacher": teacher, "features": features, "valid": valid, "w_conv": w_conv, "b_conv": b_conv, "w_head": w_head, "b_head": b_head}


def reference(teacher, features, valid, w_conv, b_conv, w_head, b_head):
    total_loss = RESIDUE_ROWS * N_ROW
    padded_pairs = jnp.pad(features, ((0, 0), (DILATION_STEP, DILATION_STEP), (DILATION_STEP, DILATION_STEP)))
    valid_f = valid.astype(jnp.float32)
    kernel = w_conv.astype(jnp.float32)
    head = w_head.astype(jnp.float32)
    count = jnp.sum(valid_f) ** 2

    def band(carry, index):
        g_conv, g_cb, g_head, g_hb, l_sum = carry
        start_row = (index * RESIDUE_ROWS).astype(jnp.int32)
        pair_window = lax.dynamic_slice_in_dim(padded_pairs, start_row, RESIDUE_ROWS + 2 * DILATION_STEP, 1)
        own = lax.dynamic_slice_in_dim(teacher, start_row, RESIDUE_ROWS, 1).astype(jnp.float32)
        other = jnp.swapaxes(lax.dynamic_slice_in_dim(teacher, start_row, RESIDUE_ROWS, 2), 1, 2).astype(jnp.float32)
        target = jax.nn.softmax(0.5 * (own + other), axis=0)
        pre = lax.conv_general_dilated(pair_window[None].astype(jnp.float32), kernel, (1, 1), "VALID",
                                       rhs_dilation=(DILATION_STEP, DILATION_STEP),
                                       dimension_numbers=("NCHW", "OIHW", "NCHW"),
                                       precision=lax.Precision.HIGHEST)[0] + b_conv[:, None, None]
        act = jax.nn.elu(pre).astype(jnp.bfloat16)
        act_f = act.astype(jnp.float32)
        logits = jnp.einsum("bc,cyx->byx", head, act_f, precision=lax.Precision.HIGHEST) + b_head[:, None, None]
        logq = jax.nn.log_softmax(logits, axis=0)
        row_valid = lax.dynamic_slice_in_dim(valid_f, start_row, RESIDUE_ROWS, 0)
        weight = row_valid[:, None] * valid_f[None, :]
        cell = -weight * jnp.sum(target * logq, axis=0)
        dlog = (weight[None] * (jnp.exp(logq) - target) / total_loss).astype(jnp.bfloat16)
        dlog_f = dlog.astype(jnp.float32)
        g_hb = g_hb + jnp.sum(dlog_f, axis=(1, 2))
        g_head = g_head + jnp.einsum("byx,cyx->bc", dlog_f, act_f, precision=lax.Precision.HIGHEST)
        back = jnp.einsum("bc,byx->cyx", head, dlog_f, precision=lax.Precision.HIGHEST)
        slope = jnp.where(pre > 0, jnp.ones_like(pre), jnp.exp(jnp.minimum(pre, 0.0)))
        dpre = (back * slope).astype(jnp.bfloat16).astype(jnp.float32)
        g_cb = g_cb + jnp.sum(dpre, axis=(1, 2))
        pair_window_float = pair_window.astype(jnp.float32)
        terms = []
        for row_offset in range(3):
            for column_offset in range(3):
                shifted_pairs = pair_window_float[:, DILATION_STEP * row_offset:DILATION_STEP * row_offset + RESIDUE_ROWS, DILATION_STEP * column_offset:DILATION_STEP * column_offset + total_loss]
                terms.append(jnp.einsum("oyx,iyx->oi", dpre, shifted_pairs, precision=lax.Precision.HIGHEST))
        stacked = jnp.stack(terms).reshape(3, 3, CH, CH).transpose(2, 3, 0, 1)
        g_conv = g_conv + stacked
        l_sum = l_sum + jnp.sum(cell)
        return (g_conv, g_cb, g_head, g_hb, l_sum), cell

    init = (jnp.zeros((CH, CH, 3, 3), jnp.float32), jnp.zeros((CH,), jnp.float32),
            jnp.zeros((BINS, CH), jnp.float32), jnp.zeros((BINS,), jnp.float32), jnp.zeros((), jnp.float32))
    final, cells = lax.scan(band, init, jnp.arange(N_ROW, dtype=jnp.int32))
    g_conv, g_cb, g_head, g_hb, l_sum = final
    pair_loss = cells.reshape(total_loss, total_loss)
    return pair_loss, l_sum / count, g_conv, g_cb, g_head, g_hb
```

```python
import functools

import jax
import jax.numpy as jnp
from jax import lax
from jax.experimental import pallas as pl
from jax.experimental.pallas import tpu as pltpu
from jax.sharding import PartitionSpec as P

STEP = 4
BLOCK = 16
HALF = 8
VMEM_BYTES = 60 * 1024 * 1024
MESH = pl.DeviceIdType.MESH
BF16, F32 = jnp.bfloat16, jnp.float32
NT = (((1,), (1,)), ((), ()))
TN = (((0,), (0,)), ((), ()))


def iota(shape, dim):
    return lax.broadcasted_iota(jnp.int32, shape, dim)


def to_column(line):
    n = line.shape[1]
    return jnp.sum(jnp.where(iota((n, n), 0) == iota((n, n), 1), jnp.broadcast_to(line, (n, n)), 0.0), axis=1, keepdims=True)


def to_line(column):
    n = column.shape[0]
    return jnp.sum(jnp.where(iota((n, n), 0) == iota((n, n), 1), jnp.broadcast_to(column, (n, n)), 0.0), axis=0, keepdims=True)


def picks(seg, cols):
    r, c = iota((32, cols), 0), iota((32, cols), 1)
    at = jnp.where(r < 16, r - 4 * seg, r - 16 - 4 * seg)
    want = jnp.where(r < 16, at, at + cols - STEP)
    return jnp.where((at >= 0) & (at < STEP) & (c == want), 1.0, 0.0).astype(BF16)


def whole_kernel(
    n_row, n_col, rows, cols, ch, bins, height,
    teacher_hbm, feat_hbm, valid_ref, w_ref, bc_ref, wh_ref, bh_ref,
    pair_ref, sums_ref,
    own, turned, mirror, hop_x, hop_y, feat, ext, strip, halo, corner, corner_halo, side, wide, pre,
    toeplitz, head, head_t, bias_c, bias_h, valid_r,
    act, logits, dlog, dpre, gw_acc, gh_acc, hb_acc, cb_acc, loss_acc,
    part_sum, row_slots, part, col_slots,
    load_sem, own_send, mirror_recv, hop_recv, fwd_send, edge_send, edge_recv, side_send, side_recv,
    rs_send, rs_recv, col_send, col_recv, ag_send, ag_recv,
):
    k = n_row // n_col
    bounce = n_col == 4 and k == 2
    blocks = rows // BLOCK
    group = (rows + 2 * STEP) // STEP
    span = 3 * ch
    tall = 6 * span
    total = rows * n_row
    low = bins // 2
    halves = ((0, low, hop_x), (low, bins - low, hop_y))
    row, col = lax.axis_index("row"), lax.axis_index("col")
    p, u = lax.div(row, k), lax.rem(row, k)
    at_home = p == col
    if bounce:
        p_y, p_x, z_y, z_x = lax.div(p, 2), lax.rem(p, 2), lax.div(col, 2), lax.rem(col, 2)
        near = (p + 1 - 2 * p_x, p + 2 - 4 * p_y)
        straight = (p_x == z_x, p_y == z_y)

    load_low = pltpu.make_async_copy(teacher_hbm.at[pl.ds(0, low)], own.at[pl.ds(0, low)], load_sem.at[0])
    load_high = pltpu.make_async_copy(teacher_hbm.at[pl.ds(low, bins - low)], own.at[pl.ds(low, bins - low)], load_sem.at[1])
    load_feat = pltpu.make_async_copy(feat_hbm, feat, load_sem.at[2])
    load_low.start()
    load_high.start()
    load_feat.start()

    barrier = pltpu.get_barrier_semaphore()

    @pl.loop(1, n_row * n_col)
    def _(o):
        peer = lax.rem(row * n_col + col + o, n_row * n_col)
        pl.semaphore_signal(
            barrier, inc=1, device_id=(lax.div(peer, n_col), lax.rem(peer, n_col)), device_id_type=MESH
        )

    def remote(src, dst, send_sem, recv_sem, device):
        return pltpu.make_async_remote_copy(
            src_ref=src, dst_ref=dst, send_sem=send_sem, recv_sem=recv_sem, device_id=device, device_id_type=MESH
        )

    def chunk(i):
        return pl.ds(pl.multiple_of(i * BLOCK, BLOCK), BLOCK)

    def direct(half, to, i):
        start, count, _ = halves[half]
        return remote(
            turned.at[to, pl.ds(start, count), chunk(i)], mirror.at[u, pl.ds(start, count), chunk(i)],
            own_send.at[half, to, i], mirror_recv.at[u, half, i], (col * k + to, p),
        )

    def stay(half, to, i):
        start, count, _ = halves[half]
        return pltpu.make_async_copy(
            turned.at[to, pl.ds(start, count), chunk(i)], mirror.at[u, pl.ds(start, count), chunk(i)],
            mirror_recv.at[u, half, i],
        )

    def first_hop(half, i):
        start, count, hop = halves[half]
        return remote(
            turned.at[:, pl.ds(start, count), chunk(i)], hop.at[:, :, chunk(i)],
            own_send.at[half, 0, i], hop_recv.at[half, i], (near[half] * k + u, col),
        )

    def second_hop(half, to, i):
        start, count, hop = halves[half]
        return remote(
            hop.at[to, :, chunk(i)], mirror.at[u, pl.ds(start, count), chunk(i)],
            fwd_send.at[half, to, i], mirror_recv.at[u, half, i], (col * k + to, near[half]),
        )

    def send_own(half, i):
        def go_direct():
            for to in range(k):
                here = at_home & (u == to)

                @pl.when(here)
                def _():
                    stay(half, to, i).start()

                @pl.when(jnp.logical_not(here))
                def _():
                    direct(half, to, i).start()

        if bounce:
            pl.when(straight[half])(go_direct)
            pl.when(jnp.logical_not(straight[half]))(lambda: first_hop(half, i).start())
        else:
            go_direct()

    def sent_own(half, i):
        def went_direct():
            for to in range(k):
                @pl.when(jnp.logical_not(at_home & (u == to)))
                def _():
                    direct(half, to, i).wait_send()

        if bounce:
            pl.when(straight[half])(went_direct)
            pl.when(jnp.logical_not(straight[half]))(lambda: first_hop(half, i).wait_send())
        else:
            went_direct()

    def forward(i):
        if bounce:
            for half in range(2):
                @pl.when(straight[half])
                def _():
                    first_hop(half, i).wait_recv()
                    for to in range(k):
                        second_hop(half, to, i).start()

    def turn(half):
        start, count, _ = halves[half]

        @pl.loop(start, start + count)
        def _(b):
            for to in range(k):
                turned[to, b] = own[b, :, to * rows : (to + 1) * rows].T

    load_low.wait()
    turn(0)
    pl.semaphore_wait(barrier, n_row * n_col - 1)

    @pl.loop(0, blocks)
    def _(i):
        send_own(0, i)

    load_high.wait()
    turn(1)

    @pl.loop(0, blocks)
    def _(i):
        send_own(1, i)

    load_feat.wait()

    @pl.loop(0, blocks)
    def _(g):
        ext[pl.ds(g * BLOCK + STEP, BLOCK)] = jnp.transpose(feat[:, chunk(g), :], (1, 0, 2))

    up = remote(ext.at[pl.ds(STEP, STEP)], ext.at[pl.ds(rows + STEP, STEP)], edge_send.at[0], edge_recv.at[0], (row - 1, col))
    down = remote(ext.at[pl.ds(rows, STEP)], ext.at[pl.ds(0, STEP)], edge_send.at[1], edge_recv.at[1], (row + 1, col))
    has_up, has_down, has_left, has_right = row > 0, row < n_row - 1, col > 0, col < n_col - 1
    pl.when(has_up)(lambda: up.start())
    pl.when(has_down)(lambda: down.start())

    def sides(held, landing, sem):
        left = remote(held.at[pl.ds(0, 16)], landing.at[pl.ds(16, 16)], side_send.at[sem], side_recv.at[sem], (row, col - 1))
        right = remote(held.at[pl.ds(16, 16)], landing.at[pl.ds(0, 16)], side_send.at[sem + 1], side_recv.at[sem + 1], (row, col + 1))
        return left, right

    quarter = rows // 4
    found = jnp.zeros((32, quarter * ch), F32)
    for s in range(4):
        lines = ext[STEP + s * quarter : STEP + (s + 1) * quarter].reshape(quarter * ch, cols)
        found = found + lax.dot_general(picks(s, cols), lines, NT, preferred_element_type=F32)
    strip[...] = found.astype(BF16)
    to_left, to_right = sides(strip, halo, 0)
    pl.when(has_left)(lambda: to_left.start())
    pl.when(has_right)(lambda: to_right.start())

    forward(0)

    toeplitz[...] = jnp.zeros_like(toeplitz)
    for n in range(4):
        for ky in range(3):
            for kx in range(3):
                start = (n + ky) * span + kx * ch
                toeplitz[n * ch : (n + 1) * ch, start : start + ch] = w_ref[3 * ky + kx]
    wide_head = HALF * ch
    tall_head = head.shape[0]
    spread = jnp.where(lax.div(iota((tall_head, bins), 0), HALF) == iota((tall_head, bins), 1), 1.0, 0.0).astype(BF16)
    tile = jnp.where(iota((ch, wide_head), 0) == lax.rem(iota((ch, wide_head), 1), ch), 1.0, 0.0).astype(BF16)

    def same_row():
        r = lax.rem(iota((tall_head, wide_head), 0), HALF)
        place = lax.div(iota((tall_head, wide_head), 1), ch)
        return r == STEP * lax.rem(place, 2) + lax.div(place, 2)

    copies = jnp.dot(spread, wh_ref[...], preferred_element_type=F32).astype(BF16)
    copies = jnp.dot(copies, tile, preferred_element_type=F32)
    head[...] = jnp.where(same_row(), copies, 0.0).astype(BF16)
    eye = jnp.where(iota((wide_head, wide_head), 0) == iota((wide_head, wide_head), 1), 1.0, 0.0).astype(BF16)
    head_t[...] = lax.dot_general(eye, head[...], NT, preferred_element_type=F32).astype(BF16)
    bias_c[...] = jnp.broadcast_to(jnp.concatenate([to_column(bc_ref[...])] * 4, axis=0), bias_c.shape)
    bias_h[...] = jnp.broadcast_to(to_column(bh_ref[...])[:, :, None], bias_h.shape)
    my_rows = valid_ref[:, pl.ds(pl.multiple_of(row * rows, rows), rows)].astype(F32)
    valid_r[...] = jnp.broadcast_to(to_column(my_rows), valid_r.shape)
    for acc in (gw_acc, gh_acc, hb_acc, cb_acc, loss_acc, dlog):
        acc[...] = jnp.zeros_like(acc)

    pl.when(has_up)(lambda: down.wait_recv())
    pl.when(has_down)(lambda: up.wait_recv())

    @pl.when(jnp.logical_not(has_up))
    def _():
        ext[0:STEP] = jnp.zeros((STEP, ch, cols), BF16)

    @pl.when(jnp.logical_not(has_down))
    def _():
        ext[rows + STEP : rows + 2 * STEP] = jnp.zeros((STEP, ch, cols), BF16)

    corner_rows = (0, 2, rows + STEP, rows + STEP + 2)
    found = jnp.zeros((32, 2 * ch), F32)
    for s, y in enumerate(corner_rows):
        found = found + lax.dot_general(picks(s, cols), ext[y : y + 2].reshape(2 * ch, cols), NT, preferred_element_type=F32)
    corner[...] = found.astype(BF16)
    corner_left, corner_right = sides(corner, corner_halo, 2)
    pl.when(has_left)(lambda: corner_left.start())
    pl.when(has_right)(lambda: corner_right.start())

    forward(1)

    def widen(e):
        edge = side[e].astype(F32)
        edge = jnp.concatenate([edge] * (cols // 128), axis=1)
        lane = iota((ch, cols), 1)
        line = ext[e]
        middle = line.astype(F32)
        left = jnp.where(lane < STEP, edge, pltpu.roll(middle, STEP, 1))
        right = jnp.where(lane >= cols - STEP, edge, pltpu.roll(middle, cols - STEP, 1))
        start = pl.multiple_of((lax.rem(e, STEP) * group + lax.div(e, STEP)) * span, span)
        wide[pl.ds(start, ch), :] = left.astype(BF16)
        wide[pl.ds(start + ch, ch), :] = line
        wide[pl.ds(start + 2 * ch, ch), :] = right.astype(BF16)

    def places(seg):
        r, c = iota((32, 128), 0), iota((32, 128), 1)
        at = jnp.where(r < 16, r - 4 * seg, r - 16 - 4 * seg)
        want = jnp.where(r < 16, at, at + 128 - STEP)
        return jnp.where((at >= 0) & (at < STEP) & (c == want), 1.0, 0.0).astype(BF16)

    def take_sides(landing, left, right):
        pl.when(has_left)(lambda: right.wait_recv())
        pl.when(has_right)(lambda: left.wait_recv())

        @pl.when(jnp.logical_not(has_left))
        def _():
            landing[0:16, :] = jnp.zeros((16, landing.shape[1]), BF16)

        @pl.when(jnp.logical_not(has_right))
        def _():
            landing[16:32, :] = jnp.zeros((16, landing.shape[1]), BF16)

    take_sides(halo, to_left, to_right)
    for s in range(4):
        put = lax.dot_general(halo[...], places(s), TN, preferred_element_type=F32).astype(BF16)
        side[STEP + s * quarter : STEP + (s + 1) * quarter] = put.reshape(quarter, ch, 128)

    for s in range(4):
        @pl.loop(STEP + s * quarter, STEP + (s + 1) * quarter, unroll=4)
        def _(e):
            widen(e)

        if s % 2:
            forward(2 + s // 2)

    take_sides(corner_halo, corner_left, corner_right)
    for s, y in enumerate(corner_rows):
        put = lax.dot_general(corner_halo[...], places(s), TN, preferred_element_type=F32).astype(BF16)
        side[y : y + 2] = put.reshape(2, ch, 128)
    for e in (*range(STEP), *range(rows + STEP, rows + 2 * STEP)):
        widen(jnp.int32(e))

    def window(r, i):
        start = pl.multiple_of((r * group + STEP * i) * span, span)
        return wide[pl.ds(start, tall), :]

    @pl.loop(0, blocks)
    def _(i):
        for r in range(STEP):
            pre[i, r] = jnp.dot(toeplitz[...], window(r, i), preferred_element_type=F32) + bias_c[...]

        @pl.when(lax.rem(i, 2) == 1)
        def _():
            forward(4 + lax.div(i, 2))

    lanes = cols // 128
    half_ch = 2 * ch

    @pl.loop(0, blocks)
    def _(i):
        for h in range(2):
            for r in range(STEP):
                v = pre[i, r, h * half_ch : (h + 1) * half_ch, :]
                a = jnp.where(v > 0, v, jnp.exp(jnp.minimum(v, 0.0)) - 1.0)
                act[r * half_ch : (r + 1) * half_ch, h * cols : (h + 1) * cols] = a.astype(BF16)
            logits[h] = jnp.dot(head[...], act[:, h * cols : (h + 1) * cols], preferred_element_type=F32)
        for source in range(k):
            for half in range(2):
                start, count, _ = halves[half]
                pltpu.make_async_copy(
                    turned.at[0, pl.ds(start, count), chunk(i)], mirror.at[source, pl.ds(start, count), chunk(i)],
                    mirror_recv.at[source, half, i],
                ).wait()
        for piece in range(lanes):
            at = pl.ds(piece * 128, 128)
            both = own[:, chunk(i), at].astype(F32) + mirror[piece * 128 // rows, :, chunk(i), :].astype(F32)
            mine = valid_ref[:, pl.ds(pl.multiple_of(col * cols + piece * 128, 128), 128)].astype(F32)
            for h in range(2):
                s = both[:, h * HALF : (h + 1) * HALF, :]
                et = jnp.exp((s - jnp.max(s, axis=0, keepdims=True)) * 0.5)
                es = jnp.sum(et, axis=0)
                lg = logits[h, 0 : bins * HALF, piece * 128 : (piece + 1) * 128].reshape(bins, HALF, 128) + bias_h[...]
                z = lg - jnp.max(lg, axis=0, keepdims=True)
                ez = jnp.exp(z)
                zs = jnp.sum(ez, axis=0)
                y = pl.multiple_of(i * BLOCK + h * HALF, HALF)
                weight = valid_r[pl.ds(y, HALF), :] * mine
                scale = 1.0 / es
                loss = weight * (jnp.log(zs) - jnp.sum(et * z, axis=0) * scale)
                pair_ref[pl.ds(y, HALF), at] = loss
                loss_acc[...] += loss
                fixed = weight * (1.0 / total)
                d = ez * (fixed * (1.0 / zs))[None] - et * (fixed * scale)[None]
                d = d.reshape(bins * HALF, 128).astype(BF16)
                dlog[0 : bins * HALF, h * cols + piece * 128 : h * cols + (piece + 1) * 128] = d
                hb_acc[...] += d.astype(F32)
        for h in range(2):
            back = jnp.dot(head_t[...], dlog[:, h * cols : (h + 1) * cols], preferred_element_type=F32)
            for r in range(STEP):
                v = pre[i, r, h * half_ch : (h + 1) * half_ch, :]
                slope = jnp.exp(jnp.minimum(v, 0.0))
                g = (back[r * half_ch : (r + 1) * half_ch, :] * slope).astype(BF16)
                dpre[h * half_ch : (h + 1) * half_ch, r * cols : (r + 1) * cols] = g
                g = g.astype(F32)
                cb_acc[...] += g[:ch] + g[ch:]
        gh_acc[...] += lax.dot_general(dlog[0:tall_head, :], act[...], NT, preferred_element_type=F32)
        windows = jnp.concatenate([window(r, i) for r in range(STEP)], axis=1)
        gw_acc[...] += lax.dot_general(windows, dpre[...], NT, preferred_element_type=F32)

    if height > 5 * ch:
        part_sum[5 * ch :, :] = jnp.zeros((height - 5 * ch, 2 * ch), F32)
    for ky in range(3):
        taps = functools.reduce(
            jnp.add, [gw_acc[(n + ky) * span : (n + ky + 1) * span, n * ch : (n + 1) * ch] for n in range(4)]
        )
        for kx in range(3):
            tap = 3 * ky + kx
            start = tap // 2 * ch
            part_sum[start : start + ch, tap % 2 * ch : (tap % 2 + 1) * ch] = taps[kx * ch : (kx + 1) * ch, :].T
    gh = jnp.where(same_row(), gh_acc[...], 0.0)
    gh = functools.reduce(jnp.add, [gh[:, n * ch : (n + 1) * ch] for n in range(HALF)])
    gh = jnp.sum(gh[0 : bins * HALF].reshape(bins, HALF, ch), axis=1)
    start = 4 * ch
    part_sum[start : start + ch, ch:] = jnp.zeros((ch, ch), F32)
    part_sum[start : start + bins, ch:] = gh
    hb = jnp.sum(jnp.sum(hb_acc[...].reshape(bins, HALF, 128), axis=1), axis=1, keepdims=True)
    part_sum[start + 40 : start + 41, ch : ch + bins] = to_line(hb)
    part_sum[start + 41 : start + 42, ch:] = to_line(jnp.sum(cb_acc[...], axis=1, keepdims=True))
    part_sum[start + 42 : start + 43, ch : ch + 1] = jnp.sum(jnp.sum(loss_acc[...], axis=0, keepdims=True), axis=1, keepdims=True)

    size = height // n_row

    def piece_of(index):
        return pl.ds(pl.multiple_of(index * size, 8), size)

    row_peers = [lax.rem(row + o, n_row) for o in range(1, n_row)]
    col_peers = [lax.rem(col + o, n_col) for o in range(1, n_col)]
    copies = [
        remote(part_sum.at[piece_of(peer)], row_slots.at[o], rs_send.at[o], rs_recv.at[o], (peer, col))
        for o, peer in enumerate(row_peers)
    ]
    for copy in copies:
        copy.start()
    added = part_sum[piece_of(row), :]
    for o, copy in enumerate(copies):
        copy.wait_recv()
        added = added + row_slots[o]
    part[0] = added
    col_slots[col] = added
    col_copies = [
        remote(part.at[0], col_slots.at[col], col_send.at[o], col_recv.at[o], (row, peer)) for o, peer in enumerate(col_peers)
    ]
    for copy in col_copies:
        copy.start()
    for copy in col_copies:
        copy.wait_recv()
    added = col_slots[0]
    for c in range(1, n_col):
        added = added + col_slots[c]
    part[1] = added
    sums_ref[piece_of(row), :] = added
    last = [
        remote(part.at[1], sums_ref.at[piece_of(row)], ag_send.at[o], ag_recv.at[o], (peer, col))
        for o, peer in enumerate(row_peers)
    ]
    for copy in last:
        copy.start()

    @pl.loop(0, blocks)
    def _(i):
        for half in range(2):
            sent_own(half, i)
            if bounce:
                @pl.when(straight[half])
                def _():
                    for to in range(k):
                        second_hop(half, to, i).wait_send()

    pl.when(has_up)(lambda: up.wait_send())
    pl.when(has_down)(lambda: down.wait_send())
    for left, right in ((to_left, to_right), (corner_left, corner_right)):
        pl.when(has_left)(lambda: left.wait_send())
        pl.when(has_right)(lambda: right.wait_send())
    for copy in copies + col_copies + last:
        copy.wait_send()
    for copy in last:
        copy.wait_recv()


def unpack_kernel(ch, bins, pair_in, sums, valid, pair_ref, loss_ref, gw_ref, cb_ref, gh_ref, hb_ref):
    pair_ref[...] = pair_in[...]
    for tap in range(9):
        start = tap // 2 * ch
        gw_ref[tap] = sums[start : start + ch, tap % 2 * ch : (tap % 2 + 1) * ch]
    start = 4 * ch
    gh_ref[...] = sums[start : start + bins, ch:]
    hb_ref[...] = sums[start + 40 : start + 41, ch : ch + bins]
    cb_ref[...] = sums[start + 41 : start + 42, ch:]
    count = jnp.sum(valid[...].astype(F32), axis=1, keepdims=True)
    loss_ref[...] = sums[start + 42 : start + 43, ch : ch + 1] / (count * count)


def on_device(teacher, features, valid, w_conv, b_conv, w_head, b_head):
    bins, rows, cols = teacher.shape
    ch = features.shape[0]
    n_row, n_col = lax.axis_size("row"), lax.axis_size("col")
    k = n_row // n_col
    blocks = rows // BLOCK
    low = bins // 2
    tall_head = -(-bins * HALF // 16) * 16
    deep_head = -(-bins * HALF // 128) * 128
    height = -(-5 * ch // (8 * n_row)) * 8 * n_row
    size = height // n_row
    quarter = rows // 4
    dma = pltpu.SemaphoreType.DMA
    vmem = pl.BlockSpec(memory_space=pltpu.VMEM)
    any_ = pl.BlockSpec(memory_space=pl.ANY)
    line = valid.reshape(1, -1)
    pair, sums = pl.pallas_call(
        functools.partial(whole_kernel, n_row, n_col, rows, cols, ch, bins, height),
        name="distil",
        out_shape=(jax.ShapeDtypeStruct((rows, cols), F32), jax.ShapeDtypeStruct((height, 2 * ch), F32)),
        in_specs=[any_, any_] + [vmem] * 5,
        out_specs=(vmem, vmem),
        scratch_shapes=[
            pltpu.VMEM((bins, rows, cols), BF16),
            pltpu.VMEM((k, bins, rows, rows), BF16),
            pltpu.VMEM((k, bins, rows, rows), BF16),
            pltpu.VMEM((k, low, rows, rows), BF16),
            pltpu.VMEM((k, bins - low, rows, rows), BF16),
            pltpu.VMEM((ch, rows, cols), BF16),
            pltpu.VMEM((rows + 2 * STEP, ch, cols), BF16),
            pltpu.VMEM((32, quarter * ch), BF16),
            pltpu.VMEM((32, quarter * ch), BF16),
            pltpu.VMEM((32, 2 * ch), BF16),
            pltpu.VMEM((32, 2 * ch), BF16),
            pltpu.VMEM((rows + 2 * STEP, ch, 128), BF16),
            pltpu.VMEM(((rows + 2 * STEP) * 3 * ch, cols), BF16),
            pltpu.VMEM((blocks, STEP, 4 * ch, cols), F32),
            pltpu.VMEM((4 * ch, 18 * ch), BF16),
            pltpu.VMEM((deep_head, HALF * ch), BF16),
            pltpu.VMEM((HALF * ch, deep_head), BF16),
            pltpu.VMEM((4 * ch, cols), F32),
            pltpu.VMEM((bins, HALF, 128), F32),
            pltpu.VMEM((rows, 128), F32),
            pltpu.VMEM((HALF * ch, 2 * cols), BF16),
            pltpu.VMEM((2, deep_head, cols), F32),
            pltpu.VMEM((deep_head, 2 * cols), BF16),
            pltpu.VMEM((4 * ch, STEP * cols), BF16),
            pltpu.VMEM((18 * ch, 4 * ch), F32),
            pltpu.VMEM((deep_head, HALF * ch), F32),
            pltpu.VMEM((bins * HALF, 128), F32),
            pltpu.VMEM((ch, cols), F32),
            pltpu.VMEM((HALF, 128), F32),
            pltpu.VMEM((height, 2 * ch), F32),
            pltpu.VMEM((n_row - 1, size, 2 * ch), F32),
            pltpu.VMEM((2, size, 2 * ch), F32),
            pltpu.VMEM((n_col, size, 2 * ch), F32),
            dma((3,)), dma((2, k, blocks)), dma((k, 2, blocks)), dma((2, blocks)), dma((2, k, blocks)),
            dma((2,)), dma((2,)), dma((4,)), dma((4,)),
            dma((n_row - 1,)), dma((n_row - 1,)), dma((n_col - 1,)), dma((n_col - 1,)), dma((n_row - 1,)), dma((n_row - 1,)),
        ],
        compiler_params=pltpu.CompilerParams(collective_id=0, has_side_effects=True, vmem_limit_bytes=VMEM_BYTES),
    )(
        teacher, features, line, jnp.transpose(w_conv, (2, 3, 0, 1)).reshape(9, ch, ch),
        b_conv.reshape(1, ch), w_head, b_head.reshape(1, bins),
    )
    pair, loss, gw, cb, gh, hb = pl.pallas_call(
        functools.partial(unpack_kernel, ch, bins),
        name="unpack",
        out_shape=(
            jax.ShapeDtypeStruct((rows, cols), F32),
            jax.ShapeDtypeStruct((1, 1), F32),
            jax.ShapeDtypeStruct((9, ch, ch), F32),
            jax.ShapeDtypeStruct((1, ch), F32),
            jax.ShapeDtypeStruct((bins, ch), F32),
            jax.ShapeDtypeStruct((1, bins), F32),
        ),
        in_specs=[vmem] * 3,
        out_specs=(vmem,) * 6,
    )(pair, sums, line)
    gw = jnp.transpose(gw.reshape(3, 3, ch, ch), (2, 3, 0, 1))
    return pair, loss.reshape(()), gw, cb.reshape(ch), gh, hb.reshape(bins)


def solution(mesh):
    in_specs = (P(None, "row", "col"), P(None, "row", "col"), P(), P(), P(), P(), P())
    out_specs = (P("row", "col"), P(), P(), P(), P(), P())
    return jax.shard_map(
        on_device, mesh=mesh, in_specs=in_specs, out_specs=out_specs, check_vma=False
    )
```

```python
import functools

import jax
import jax.numpy as jnp
from jax import lax
from jax.experimental import pallas as pl
from jax.experimental.pallas import tpu as pltpu
from jax.sharding import PartitionSpec as P

STEP = 4
BLOCK = 16
HALF = 8
AHEAD = 2
VMEM_BYTES = 60 * 1024 * 1024
MESH = pl.DeviceIdType.MESH
BF16, F32 = jnp.bfloat16, jnp.float32
NT = (((1,), (1,)), ((), ()))
TN = (((0,), (0,)), ((), ()))


def iota(shape, dim):
    return lax.broadcasted_iota(jnp.int32, shape, dim)


def to_column(line):
    n = line.shape[1]
    return jnp.sum(jnp.where(iota((n, n), 0) == iota((n, n), 1), jnp.broadcast_to(line, (n, n)), 0.0), axis=1, keepdims=True)


def to_line(column):
    n = column.shape[0]
    return jnp.sum(jnp.where(iota((n, n), 0) == iota((n, n), 1), jnp.broadcast_to(column, (n, n)), 0.0), axis=0, keepdims=True)


def picks(seg, cols):
    r, c = iota((32, cols), 0), iota((32, cols), 1)
    at = jnp.where(r < 16, r - 4 * seg, r - 16 - 4 * seg)
    want = jnp.where(r < 16, at, at + cols - STEP)
    return jnp.where((at >= 0) & (at < STEP) & (c == want), 1.0, 0.0).astype(BF16)


def whole_kernel(
    n_row, n_col, rows, cols, ch, bins, height,
    teacher_hbm, feat_hbm, valid_ref, w_ref, bc_ref, wh_ref, bh_ref,
    pair_ref, sums_ref,
    own, turned, mirror, hop_x, hop_y, feat, ext, strip, halo, corner, corner_halo, side, wide, pre,
    toeplitz, head, head_t, bias_c, bias_h, valid_r,
    act, logits, dlog, dpre, gw_acc, gh_acc, hb_acc, cb_acc, loss_acc,
    part_sum, row_slots, part, col_slots,
    load_sem, own_send, mirror_recv, hop_recv, fwd_send, edge_send, edge_recv, side_send, side_recv,
    rs_send, rs_recv, col_send, col_recv, ag_send, ag_recv,
):
    k = n_row // n_col
    bounce = n_col == 4 and k == 2
    blocks = rows // BLOCK
    group = (rows + 2 * STEP) // STEP
    span = 3 * ch
    tall = 6 * span
    total = rows * n_row
    low = bins // 2
    halves = ((0, low, hop_x), (low, bins - low, hop_y))
    row, col = lax.axis_index("row"), lax.axis_index("col")
    p, u = lax.div(row, k), lax.rem(row, k)
    at_home = p == col
    if bounce:
        p_y, p_x, z_y, z_x = lax.div(p, 2), lax.rem(p, 2), lax.div(col, 2), lax.rem(col, 2)
        near = (p + 1 - 2 * p_x, p + 2 - 4 * p_y)
        straight = (p_x == z_x, p_y == z_y)

    quarter = rows // 4
    loads = [
        pltpu.make_async_copy(feat_hbm.at[:, pl.ds(s * quarter, quarter)], feat.at[:, pl.ds(s * quarter, quarter)], load_sem.at[s])
        for s in range(4)
    ]
    load_own = pltpu.make_async_copy(teacher_hbm, own, load_sem.at[4])
    load_own.start()
    for load in loads:
        load.start()

    barrier = pltpu.get_barrier_semaphore()

    @pl.loop(1, n_row * n_col)
    def _(o):
        peer = lax.rem(row * n_col + col + o, n_row * n_col)
        pl.semaphore_signal(
            barrier, inc=1, device_id=(lax.div(peer, n_col), lax.rem(peer, n_col)), device_id_type=MESH
        )

    def remote(src, dst, send_sem, recv_sem, device):
        return pltpu.make_async_remote_copy(
            src_ref=src, dst_ref=dst, send_sem=send_sem, recv_sem=recv_sem, device_id=device, device_id_type=MESH
        )

    def chunk(i):
        return pl.ds(pl.multiple_of(i * BLOCK, BLOCK), BLOCK)

    def direct(half, to, i):
        start, count, _ = halves[half]
        return remote(
            turned.at[to, pl.ds(start, count), chunk(i)], mirror.at[u, pl.ds(start, count), chunk(i)],
            own_send.at[half, to, i], mirror_recv.at[u, half, i], (col * k + to, p),
        )

    def stay(half, to, i):
        start, count, _ = halves[half]
        return pltpu.make_async_copy(
            turned.at[to, pl.ds(start, count), chunk(i)], mirror.at[u, pl.ds(start, count), chunk(i)],
            mirror_recv.at[u, half, i],
        )

    def first_hop(half, i):
        start, count, hop = halves[half]
        return remote(
            turned.at[:, pl.ds(start, count), chunk(i)], hop.at[:, :, chunk(i)],
            own_send.at[half, 0, i], hop_recv.at[half, i], (near[half] * k + u, col),
        )

    def second_hop(half, to, i):
        start, count, hop = halves[half]
        return remote(
            hop.at[to, :, chunk(i)], mirror.at[u, pl.ds(start, count), chunk(i)],
            fwd_send.at[half, to, i], mirror_recv.at[u, half, i], (col * k + to, near[half]),
        )

    def send_own(half, i):
        def go_direct():
            for to in range(k):
                here = at_home & (u == to)

                @pl.when(here)
                def _():
                    stay(half, to, i).start()

                @pl.when(jnp.logical_not(here))
                def _():
                    direct(half, to, i).start()

        if bounce:
            pl.when(straight[half])(go_direct)
            pl.when(jnp.logical_not(straight[half]))(lambda: first_hop(half, i).start())
        else:
            go_direct()

    def sent_own(half, i):
        def went_direct():
            for to in range(k):
                @pl.when(jnp.logical_not(at_home & (u == to)))
                def _():
                    direct(half, to, i).wait_send()

        if bounce:
            pl.when(straight[half])(went_direct)
            pl.when(jnp.logical_not(straight[half]))(lambda: first_hop(half, i).wait_send())
        else:
            went_direct()

    def tick(i):
        if bounce:
            for half in range(2):
                @pl.when(straight[half])
                def _():
                    first_hop(half, i).wait_recv()
                    for to in range(k):
                        second_hop(half, to, i).start()

        @pl.when(i + AHEAD < blocks)
        def _():
            for half in range(2):
                send_own(half, i + AHEAD)

    has_up, has_down, has_left, has_right = row > 0, row < n_row - 1, col > 0, col < n_col - 1
    has_row, has_col = (has_up, has_down), (has_left, has_right)

    for v in range(2):
        @pl.when(jnp.logical_not(has_row[v]))
        def _():
            ext[v * (rows + STEP) : v * (rows + STEP) + STEP] = jnp.zeros((STEP, ch, cols), BF16)

        @pl.when(jnp.logical_not(has_col[v]))
        def _():
            halo[v * 16 : (v + 1) * 16, :] = jnp.zeros((16, quarter * ch), BF16)

        for h in range(2):
            @pl.when(jnp.logical_not(has_row[v] & has_col[h]))
            def _():
                corner_halo[(2 * v + h) * 16 : (2 * v + h + 1) * 16, :] = jnp.zeros((16, 2 * ch), BF16)

    load_own.wait()

    @pl.loop(0, bins)
    def _(b):
        for to in range(k):
            turned[to, b] = own[b, :, to * rows : (to + 1) * rows].T

    pl.semaphore_wait(barrier, n_row * n_col - 1)

    for half in range(2):
        send_own(half, 0)

    edges = [
        remote(
            ext.at[pl.ds(STEP + v * (rows - STEP), STEP)], ext.at[pl.ds((1 - v) * (rows + STEP), STEP)],
            edge_send.at[v], edge_recv.at[v], (row + 2 * v - 1, col),
        )
        for v in range(2)
    ]
    lines = [
        remote(
            strip.at[pl.ds(h * 16, 16)], halo.at[pl.ds((1 - h) * 16, 16)],
            side_send.at[h], side_recv.at[h], (row, col + 2 * h - 1),
        )
        for h in range(2)
    ]
    corners = [
        [
            remote(
                corner.at[pl.ds((2 * v + h) * 16, 16)], corner_halo.at[pl.ds((3 - 2 * v - h) * 16, 16)],
                side_send.at[2 + 2 * v + h], side_recv.at[2 + 2 * v + h], (row + 2 * v - 1, col + 2 * h - 1),
            )
            for h in range(2)
        ]
        for v in range(2)
    ]

    def swap(g):
        ext[g * BLOCK + STEP : (g + 1) * BLOCK + STEP] = jnp.transpose(feat[:, g * BLOCK : (g + 1) * BLOCK, :], (1, 0, 2))

    for load in loads:
        load.wait()
    for v in range(2):
        swap(v * (blocks - 1))
        pl.when(has_row[v])(lambda: edges[v].start())
        found = jnp.zeros((32, 2 * ch), F32)
        for s in range(2):
            y = STEP + v * (rows - STEP) + 2 * s
            found = found + lax.dot_general(picks(s, cols), ext[y : y + 2].reshape(2 * ch, cols), NT, preferred_element_type=F32)
        corner[v * 32 : (v + 1) * 32, :] = found.astype(BF16)
        for h in range(2):
            pl.when(has_row[v] & has_col[h])(lambda: corners[v][h].start())
    for g in range(1, blocks - 1):
        swap(g)
    found = jnp.zeros((32, quarter * ch), F32)
    for s in range(4):
        own_lines = ext[STEP + s * quarter : STEP + (s + 1) * quarter].reshape(quarter * ch, cols)
        found = found + lax.dot_general(picks(s, cols), own_lines, NT, preferred_element_type=F32)
    strip[...] = found.astype(BF16)
    for h in range(2):
        pl.when(has_col[h])(lambda: lines[h].start())
    for i in range(1, AHEAD):
        for half in range(2):
            send_own(half, i)
    tick(0)

    toeplitz[...] = jnp.zeros_like(toeplitz)
    for n in range(4):
        for ky in range(3):
            for kx in range(3):
                start = (n + ky) * span + kx * ch
                toeplitz[n * ch : (n + 1) * ch, start : start + ch] = w_ref[3 * ky + kx]
    wide_head = HALF * ch
    tall_head = head.shape[0]
    spread = jnp.where(lax.div(iota((tall_head, bins), 0), HALF) == iota((tall_head, bins), 1), 1.0, 0.0).astype(BF16)
    tile = jnp.where(iota((ch, wide_head), 0) == lax.rem(iota((ch, wide_head), 1), ch), 1.0, 0.0).astype(BF16)

    def same_row():
        r = lax.rem(iota((tall_head, wide_head), 0), HALF)
        place = lax.div(iota((tall_head, wide_head), 1), ch)
        return r == STEP * lax.rem(place, 2) + lax.div(place, 2)

    copies = jnp.dot(spread, wh_ref[...], preferred_element_type=F32).astype(BF16)
    copies = jnp.dot(copies, tile, preferred_element_type=F32)
    head[...] = jnp.where(same_row(), copies, 0.0).astype(BF16)
    eye = jnp.where(iota((wide_head, wide_head), 0) == iota((wide_head, wide_head), 1), 1.0, 0.0).astype(BF16)
    head_t[...] = jnp.zeros_like(head_t)
    head_t[:, 0:tall_head] = lax.dot_general(eye, head[...], NT, preferred_element_type=F32).astype(BF16)
    bias_c[...] = jnp.broadcast_to(jnp.concatenate([to_column(bc_ref[...])] * 4, axis=0), bias_c.shape)
    bias_h[...] = jnp.broadcast_to(to_column(bh_ref[...])[:, :, None], bias_h.shape)
    my_rows = valid_ref[:, pl.ds(pl.multiple_of(row * rows, rows), rows)].astype(F32)
    valid_r[...] = jnp.broadcast_to(to_column(my_rows), valid_r.shape)
    for acc in (gw_acc, gh_acc, hb_acc, cb_acc, loss_acc, dlog):
        acc[...] = jnp.zeros_like(acc)

    tick(1)

    def widen(e):
        edge = side[e].astype(F32)
        edge = jnp.concatenate([edge] * (cols // 128), axis=1)
        lane = iota((ch, cols), 1)
        line = ext[e]
        middle = line.astype(F32)
        left = jnp.where(lane < STEP, edge, pltpu.roll(middle, STEP, 1))
        right = jnp.where(lane >= cols - STEP, edge, pltpu.roll(middle, cols - STEP, 1))
        start = pl.multiple_of((lax.rem(e, STEP) * group + lax.div(e, STEP)) * span, span)
        wide[pl.ds(start, ch), :] = left.astype(BF16)
        wide[pl.ds(start + ch, ch), :] = line
        wide[pl.ds(start + 2 * ch, ch), :] = right.astype(BF16)

    def places(seg):
        r, c = iota((32, 128), 0), iota((32, 128), 1)
        at = jnp.where(r < 16, r - 4 * seg, r - 16 - 4 * seg)
        want = jnp.where(r < 16, at, at + 128 - STEP)
        return jnp.where((at >= 0) & (at < STEP) & (c == want), 1.0, 0.0).astype(BF16)

    for v in range(2):
        pl.when(has_col[v])(lambda: lines[1 - v].wait_recv())
        pl.when(has_row[v])(lambda: edges[1 - v].wait_recv())
        for h in range(2):
            pl.when(has_row[v] & has_col[h])(lambda: corners[1 - v][1 - h].wait_recv())
    for s in range(4):
        put = lax.dot_general(halo[...], places(s), TN, preferred_element_type=F32).astype(BF16)
        side[STEP + s * quarter : STEP + (s + 1) * quarter] = put.reshape(quarter, ch, 128)

    for s in range(4):
        @pl.loop(STEP + s * quarter, STEP + (s + 1) * quarter, unroll=4)
        def _(e):
            widen(e)

        if s % 2:
            tick(2 + s // 2)

    for v in range(2):
        for s in range(2):
            y = v * (rows + STEP) + 2 * s
            put = lax.dot_general(corner_halo[v * 32 : (v + 1) * 32, :], places(s), TN, preferred_element_type=F32).astype(BF16)
            side[y : y + 2] = put.reshape(2, ch, 128)
    for e in (*range(STEP), *range(rows + STEP, rows + 2 * STEP)):
        widen(jnp.int32(e))

    def window(r, i):
        start = pl.multiple_of((r * group + STEP * i) * span, span)
        return wide[pl.ds(start, tall), :]

    @pl.loop(0, blocks)
    def _(i):
        for r in range(STEP):
            pre[i, r] = jnp.dot(toeplitz[...], window(r, i), preferred_element_type=F32) + bias_c[...]

        @pl.when(lax.rem(i, 2) == 1)
        def _():
            tick(4 + lax.div(i, 2))

    for i in range(4 + blocks // 2, blocks):
        tick(i)

    lanes = cols // 128
    half_ch = 2 * ch

    @pl.loop(0, blocks)
    def _(i):
        for h in range(2):
            for r in range(STEP):
                v = pre[i, r, h * half_ch : (h + 1) * half_ch, :]
                a = jnp.where(v > 0, v, jnp.exp(jnp.minimum(v, 0.0)) - 1.0)
                act[r * half_ch : (r + 1) * half_ch, h * cols : (h + 1) * cols] = a.astype(BF16)
            logits[h] = jnp.dot(head[...], act[:, h * cols : (h + 1) * cols], preferred_element_type=F32)
        for source in range(k):
            for half in range(2):
                start, count, _ = halves[half]
                pltpu.make_async_copy(
                    turned.at[0, pl.ds(start, count), chunk(i)], mirror.at[source, pl.ds(start, count), chunk(i)],
                    mirror_recv.at[source, half, i],
                ).wait()
        for piece in range(lanes):
            at = pl.ds(piece * 128, 128)
            both = own[:, chunk(i), at].astype(F32) + mirror[piece * 128 // rows, :, chunk(i), :].astype(F32)
            mine = valid_ref[:, pl.ds(pl.multiple_of(col * cols + piece * 128, 128), 128)].astype(F32)
            for h in range(2):
                s = both[:, h * HALF : (h + 1) * HALF, :]
                et = jnp.exp((s - jnp.max(s, axis=0, keepdims=True)) * 0.5)
                es = jnp.sum(et, axis=0)
                lg = logits[h, 0 : bins * HALF, piece * 128 : (piece + 1) * 128].reshape(bins, HALF, 128) + bias_h[...]
                z = lg - jnp.max(lg, axis=0, keepdims=True)
                ez = jnp.exp(z)
                zs = jnp.sum(ez, axis=0)
                y = pl.multiple_of(i * BLOCK + h * HALF, HALF)
                weight = valid_r[pl.ds(y, HALF), :] * mine
                scale = 1.0 / es
                loss = weight * (jnp.log(zs) - jnp.sum(et * z, axis=0) * scale)
                pair_ref[pl.ds(y, HALF), at] = loss
                loss_acc[...] += loss
                fixed = weight * (1.0 / total)
                d = ez * (fixed * (1.0 / zs))[None] - et * (fixed * scale)[None]
                d = d.reshape(bins * HALF, 128).astype(BF16)
                dlog[0 : bins * HALF, h * cols + piece * 128 : h * cols + (piece + 1) * 128] = d
                hb_acc[...] += d.astype(F32)
        for h in range(2):
            back = jnp.dot(head_t[...], dlog[:, h * cols : (h + 1) * cols], preferred_element_type=F32)
            for r in range(STEP):
                v = pre[i, r, h * half_ch : (h + 1) * half_ch, :]
                slope = jnp.exp(jnp.minimum(v, 0.0))
                g = (back[r * half_ch : (r + 1) * half_ch, :] * slope).astype(BF16)
                dpre[h * half_ch : (h + 1) * half_ch, r * cols : (r + 1) * cols] = g
                g = g.astype(F32)
                cb_acc[...] += g[:ch] + g[ch:]
        gh_acc[...] += lax.dot_general(dlog[0:tall_head, :], act[...], NT, preferred_element_type=F32)
        windows = jnp.concatenate([window(r, i) for r in range(STEP)], axis=1)
        gw_acc[...] += lax.dot_general(windows, dpre[...], NT, preferred_element_type=F32)

    if height > 5 * ch:
        part_sum[5 * ch :, :] = jnp.zeros((height - 5 * ch, 2 * ch), F32)
    for ky in range(3):
        taps = functools.reduce(
            jnp.add, [gw_acc[(n + ky) * span : (n + ky + 1) * span, n * ch : (n + 1) * ch] for n in range(4)]
        )
        for kx in range(3):
            tap = 3 * ky + kx
            start = tap // 2 * ch
            part_sum[start : start + ch, tap % 2 * ch : (tap % 2 + 1) * ch] = taps[kx * ch : (kx + 1) * ch, :].T
    gh = jnp.where(same_row(), gh_acc[...], 0.0)
    gh = functools.reduce(jnp.add, [gh[:, n * ch : (n + 1) * ch] for n in range(HALF)])
    gh = jnp.sum(gh[0 : bins * HALF].reshape(bins, HALF, ch), axis=1)
    start = 4 * ch
    part_sum[start : start + ch, ch:] = jnp.zeros((ch, ch), F32)
    part_sum[start : start + bins, ch:] = gh
    hb = jnp.sum(jnp.sum(hb_acc[...].reshape(bins, HALF, 128), axis=1), axis=1, keepdims=True)
    part_sum[start + 40 : start + 41, ch : ch + bins] = to_line(hb)
    part_sum[start + 41 : start + 42, ch:] = to_line(jnp.sum(cb_acc[...], axis=1, keepdims=True))
    part_sum[start + 42 : start + 43, ch : ch + 1] = jnp.sum(jnp.sum(loss_acc[...], axis=0, keepdims=True), axis=1, keepdims=True)

    size = height // n_row

    def piece_of(index):
        return pl.ds(pl.multiple_of(index * size, 8), size)

    row_peers = [lax.rem(row + o, n_row) for o in range(1, n_row)]
    col_peers = [lax.rem(col + o, n_col) for o in range(1, n_col)]
    copies = [
        remote(part_sum.at[piece_of(peer)], row_slots.at[o], rs_send.at[o], rs_recv.at[o], (peer, col))
        for o, peer in enumerate(row_peers)
    ]
    for copy in copies:
        copy.start()
    added = part_sum[piece_of(row), :]
    for o, copy in enumerate(copies):
        copy.wait_recv()
        added = added + row_slots[o]
    part[0] = added
    col_slots[col] = added
    col_copies = [
        remote(part.at[0], col_slots.at[col], col_send.at[o], col_recv.at[o], (row, peer)) for o, peer in enumerate(col_peers)
    ]
    for copy in col_copies:
        copy.start()
    for copy in col_copies:
        copy.wait_recv()
    added = col_slots[0]
    for c in range(1, n_col):
        added = added + col_slots[c]
    part[1] = added
    sums_ref[piece_of(row), :] = added
    last = [
        remote(part.at[1], sums_ref.at[piece_of(row)], ag_send.at[o], ag_recv.at[o], (peer, col))
        for o, peer in enumerate(row_peers)
    ]
    for copy in last:
        copy.start()

    @pl.loop(0, blocks)
    def _(i):
        for half in range(2):
            sent_own(half, i)
            if bounce:
                @pl.when(straight[half])
                def _():
                    for to in range(k):
                        second_hop(half, to, i).wait_send()

    for v in range(2):
        pl.when(has_row[v])(lambda: edges[v].wait_send())
        pl.when(has_col[v])(lambda: lines[v].wait_send())
        for h in range(2):
            pl.when(has_row[v] & has_col[h])(lambda: corners[v][h].wait_send())
    for copy in copies + col_copies + last:
        copy.wait_send()
    for copy in last:
        copy.wait_recv()


def unpack_kernel(ch, bins, pair_in, sums, valid, pair_ref, loss_ref, gw_ref, cb_ref, gh_ref, hb_ref):
    pair_ref[...] = pair_in[...]
    for tap in range(9):
        start = tap // 2 * ch
        gw_ref[tap] = sums[start : start + ch, tap % 2 * ch : (tap % 2 + 1) * ch]
    start = 4 * ch
    gh_ref[...] = sums[start : start + bins, ch:]
    hb_ref[...] = sums[start + 40 : start + 41, ch : ch + bins]
    cb_ref[...] = sums[start + 41 : start + 42, ch:]
    count = jnp.sum(valid[...].astype(F32), axis=1, keepdims=True)
    loss_ref[...] = sums[start + 42 : start + 43, ch : ch + 1] / (count * count)


def on_device(teacher, features, valid, w_conv, b_conv, w_head, b_head):
    bins, rows, cols = teacher.shape
    ch = features.shape[0]
    n_row, n_col = lax.axis_size("row"), lax.axis_size("col")
    k = n_row // n_col
    blocks = rows // BLOCK
    low = bins // 2
    tall_head = -(-bins * HALF // 16) * 16
    deep_head = -(-bins * HALF // 128) * 128
    height = -(-5 * ch // (8 * n_row)) * 8 * n_row
    size = height // n_row
    quarter = rows // 4
    dma = pltpu.SemaphoreType.DMA
    vmem = pl.BlockSpec(memory_space=pltpu.VMEM)
    any_ = pl.BlockSpec(memory_space=pl.ANY)
    line = valid.reshape(1, -1)
    pair, sums = pl.pallas_call(
        functools.partial(whole_kernel, n_row, n_col, rows, cols, ch, bins, height),
        name="distil",
        out_shape=(jax.ShapeDtypeStruct((rows, cols), F32), jax.ShapeDtypeStruct((height, 2 * ch), F32)),
        in_specs=[any_, any_] + [vmem] * 5,
        out_specs=(vmem, vmem),
        scratch_shapes=[
            pltpu.VMEM((bins, rows, cols), BF16),
            pltpu.VMEM((k, bins, rows, rows), BF16),
            pltpu.VMEM((k, bins, rows, rows), BF16),
            pltpu.VMEM((k, low, rows, rows), BF16),
            pltpu.VMEM((k, bins - low, rows, rows), BF16),
            pltpu.VMEM((ch, rows, cols), BF16),
            pltpu.VMEM((rows + 2 * STEP, ch, cols), BF16),
            pltpu.VMEM((32, quarter * ch), BF16),
            pltpu.VMEM((32, quarter * ch), BF16),
            pltpu.VMEM((64, 2 * ch), BF16),
            pltpu.VMEM((64, 2 * ch), BF16),
            pltpu.VMEM((rows + 2 * STEP, ch, 128), BF16),
            pltpu.VMEM(((rows + 2 * STEP) * 3 * ch, cols), BF16),
            pltpu.VMEM((blocks, STEP, 4 * ch, cols), F32),
            pltpu.VMEM((4 * ch, 18 * ch), BF16),
            pltpu.VMEM((tall_head, HALF * ch), BF16),
            pltpu.VMEM((HALF * ch, deep_head), BF16),
            pltpu.VMEM((4 * ch, cols), F32),
            pltpu.VMEM((bins, HALF, 128), F32),
            pltpu.VMEM((rows, 128), F32),
            pltpu.VMEM((HALF * ch, 2 * cols), BF16),
            pltpu.VMEM((2, tall_head, cols), F32),
            pltpu.VMEM((deep_head, 2 * cols), BF16),
            pltpu.VMEM((4 * ch, STEP * cols), BF16),
            pltpu.VMEM((18 * ch, 4 * ch), F32),
            pltpu.VMEM((tall_head, HALF * ch), F32),
            pltpu.VMEM((bins * HALF, 128), F32),
            pltpu.VMEM((ch, cols), F32),
            pltpu.VMEM((HALF, 128), F32),
            pltpu.VMEM((height, 2 * ch), F32),
            pltpu.VMEM((n_row - 1, size, 2 * ch), F32),
            pltpu.VMEM((2, size, 2 * ch), F32),
            pltpu.VMEM((n_col, size, 2 * ch), F32),
            dma((5,)), dma((2, k, blocks)), dma((k, 2, blocks)), dma((2, blocks)), dma((2, k, blocks)),
            dma((2,)), dma((2,)), dma((6,)), dma((6,)),
            dma((n_row - 1,)), dma((n_row - 1,)), dma((n_col - 1,)), dma((n_col - 1,)), dma((n_row - 1,)), dma((n_row - 1,)),
        ],
        compiler_params=pltpu.CompilerParams(collective_id=0, has_side_effects=True, vmem_limit_bytes=VMEM_BYTES),
    )(
        teacher, features, line, jnp.transpose(w_conv, (2, 3, 0, 1)).reshape(9, ch, ch),
        b_conv.reshape(1, ch), w_head, b_head.reshape(1, bins),
    )
    pair, loss, gw, cb, gh, hb = pl.pallas_call(
        functools.partial(unpack_kernel, ch, bins),
        name="unpack",
        out_shape=(
            jax.ShapeDtypeStruct((rows, cols), F32),
            jax.ShapeDtypeStruct((1, 1), F32),
            jax.ShapeDtypeStruct((9, ch, ch), F32),
            jax.ShapeDtypeStruct((1, ch), F32),
            jax.ShapeDtypeStruct((bins, ch), F32),
            jax.ShapeDtypeStruct((1, bins), F32),
        ),
        in_specs=[vmem] * 3,
        out_specs=(vmem,) * 6,
    )(pair, sums, line)
    gw = jnp.transpose(gw.reshape(3, 3, ch, ch), (2, 3, 0, 1))
    return pair, loss.reshape(()), gw, cb.reshape(ch), gh, hb.reshape(bins)


def solution(mesh):
    in_specs = (P(None, "row", "col"), P(None, "row", "col"), P(), P(), P(), P(), P())
    out_specs = (P("row", "col"), P(), P(), P(), P(), P())
    return jax.shard_map(
        on_device, mesh=mesh, in_specs=in_specs, out_specs=out_specs, check_vma=False
    )
```

```python
import functools

import jax
import jax.numpy as jnp
from jax import lax
from jax.experimental import pallas as pl
from jax.experimental.pallas import tpu as pltpu
from jax.sharding import PartitionSpec as P

STEP = 4
BLOCK = 16
HALF = 8
AHEAD = 2
VMEM_BYTES = 60 * 1024 * 1024
MESH = pl.DeviceIdType.MESH
BF16, F32 = jnp.bfloat16, jnp.float32
NT = (((1,), (1,)), ((), ()))
TN = (((0,), (0,)), ((), ()))


def iota(shape, dim):
    return lax.broadcasted_iota(jnp.int32, shape, dim)


def to_column(line):
    n = line.shape[1]
    return jnp.sum(jnp.where(iota((n, n), 0) == iota((n, n), 1), jnp.broadcast_to(line, (n, n)), 0.0), axis=1, keepdims=True)


def to_line(column):
    n = column.shape[0]
    return jnp.sum(jnp.where(iota((n, n), 0) == iota((n, n), 1), jnp.broadcast_to(column, (n, n)), 0.0), axis=0, keepdims=True)


def picks(seg, cols):
    r, c = iota((32, cols), 0), iota((32, cols), 1)
    at = jnp.where(r < 16, r - 4 * seg, r - 16 - 4 * seg)
    want = jnp.where(r < 16, at, at + cols - STEP)
    return jnp.where((at >= 0) & (at < STEP) & (c == want), 1.0, 0.0).astype(BF16)


def whole_kernel(
    n_row, n_col, rows, cols, ch, bins, height,
    teacher_hbm, feat_hbm, *rest,
):
    small_hbm, rest = rest[:5], rest[5:]
    (
        pair_ref, sums_ref,
        own, turned, mirror, hop_x, hop_y, feat, ext, strip, halo, corner, corner_halo, side, wide, pre,
        toeplitz, head, head_t, bias_c, bias_h, valid_r,
        act, logits, dlog, dpre, gw_acc, gh_acc, hb_acc, cb_acc, loss_acc,
        part_sum, row_slots, part, col_slots,
        valid_ref, w_ref, bc_ref, wh_ref, bh_ref, small_sem,
        load_sem, own_send, mirror_recv, hop_recv, fwd_send, edge_send, edge_recv, side_send, side_recv,
        rs_send, rs_recv, col_send, col_recv, ag_send, ag_recv,
    ) = rest
    k = n_row // n_col
    bounce = n_col == 4 and k == 2
    blocks = rows // BLOCK
    group = (rows + 2 * STEP) // STEP
    span = 3 * ch
    tall = 6 * span
    total = rows * n_row
    low = bins // 2
    halves = ((0, low, hop_x), (low, bins - low, hop_y))
    row, col = lax.axis_index("row"), lax.axis_index("col")
    p, u = lax.div(row, k), lax.rem(row, k)
    at_home = p == col
    if bounce:
        p_y, p_x, z_y, z_x = lax.div(p, 2), lax.rem(p, 2), lax.div(col, 2), lax.rem(col, 2)
        near = (p + 1 - 2 * p_x, p + 2 - 4 * p_y)
        straight = (p_x == z_x, p_y == z_y)

    barrier = pltpu.get_barrier_semaphore()

    @pl.loop(1, n_row * n_col)
    def _(o):
        peer = lax.rem(row * n_col + col + o, n_row * n_col)
        pl.semaphore_signal(
            barrier, inc=1, device_id=(lax.div(peer, n_col), lax.rem(peer, n_col)), device_id_type=MESH
        )

    quarter = rows // 4
    loads = [
        pltpu.make_async_copy(feat_hbm.at[:, pl.ds(s * quarter, quarter)], feat.at[:, pl.ds(s * quarter, quarter)], load_sem.at[s])
        for s in range(4)
    ]
    load_own = [
        pltpu.make_async_copy(teacher_hbm.at[pl.ds(start, count)], own.at[pl.ds(start, count)], load_sem.at[4 + half])
        for half, (start, count, _) in enumerate(halves)
    ]
    load_own[1].start()
    load_own[0].start()
    for load in loads:
        load.start()
    small = [
        pltpu.make_async_copy(src, dst, small_sem.at[n])
        for n, (src, dst) in enumerate(zip(small_hbm, (valid_ref, w_ref, bc_ref, wh_ref, bh_ref)))
    ]
    for load in small:
        load.start()

    def remote(src, dst, send_sem, recv_sem, device):
        return pltpu.make_async_remote_copy(
            src_ref=src, dst_ref=dst, send_sem=send_sem, recv_sem=recv_sem, device_id=device, device_id_type=MESH
        )

    def chunk(i):
        return pl.ds(pl.multiple_of(i * BLOCK, BLOCK), BLOCK)

    def direct(half, to, i):
        start, count, _ = halves[half]
        return remote(
            turned.at[to, pl.ds(start, count), chunk(i)], mirror.at[u, pl.ds(start, count), chunk(i)],
            own_send.at[half, to, i], mirror_recv.at[u, half, i], (col * k + to, p),
        )

    def stay(half, to, i):
        start, count, _ = halves[half]
        return pltpu.make_async_copy(
            turned.at[to, pl.ds(start, count), chunk(i)], mirror.at[u, pl.ds(start, count), chunk(i)],
            mirror_recv.at[u, half, i],
        )

    def first_hop(half, i):
        start, count, hop = halves[half]
        return remote(
            turned.at[:, pl.ds(start, count), chunk(i)], hop.at[:, :, chunk(i)],
            own_send.at[half, 0, i], hop_recv.at[half, i], (near[half] * k + u, col),
        )

    def second_hop(half, to, i):
        start, count, hop = halves[half]
        return remote(
            hop.at[to, :, chunk(i)], mirror.at[u, pl.ds(start, count), chunk(i)],
            fwd_send.at[half, to, i], mirror_recv.at[u, half, i], (col * k + to, near[half]),
        )

    def send_own(half, i):
        def go_direct():
            for to in range(k):
                here = at_home & (u == to)

                @pl.when(here)
                def _():
                    stay(half, to, i).start()

                @pl.when(jnp.logical_not(here))
                def _():
                    direct(half, to, i).start()

        if bounce:
            pl.when(straight[half])(go_direct)
            pl.when(jnp.logical_not(straight[half]))(lambda: first_hop(half, i).start())
        else:
            go_direct()

    def sent_own(half, i):
        def went_direct():
            for to in range(k):
                @pl.when(jnp.logical_not(at_home & (u == to)))
                def _():
                    direct(half, to, i).wait_send()

        if bounce:
            pl.when(straight[half])(went_direct)
            pl.when(jnp.logical_not(straight[half]))(lambda: first_hop(half, i).wait_send())
        else:
            went_direct()

    def tick(i):
        if bounce:
            for half in (1, 0):
                @pl.when(straight[half])
                def _():
                    first_hop(half, i).wait_recv()
                    for to in range(k):
                        second_hop(half, to, i).start()

        @pl.when(i + AHEAD < blocks)
        def _():
            for half in (1, 0):
                send_own(half, i + AHEAD)

    has_up, has_down, has_left, has_right = row > 0, row < n_row - 1, col > 0, col < n_col - 1
    has_row, has_col = (has_up, has_down), (has_left, has_right)

    for v in range(2):
        @pl.when(jnp.logical_not(has_row[v]))
        def _():
            ext[v * (rows + STEP) : v * (rows + STEP) + STEP] = jnp.zeros((STEP, ch, cols), BF16)

        @pl.when(jnp.logical_not(has_col[v]))
        def _():
            halo[v * 16 : (v + 1) * 16, :] = jnp.zeros((16, quarter * ch), BF16)

        for h in range(2):
            @pl.when(jnp.logical_not(has_row[v] & has_col[h]))
            def _():
                corner_halo[(2 * v + h) * 16 : (2 * v + h + 1) * 16, :] = jnp.zeros((16, 2 * ch), BF16)

    for half in (1, 0):
        start, count, _ = halves[half]
        load_own[half].wait()

        @pl.loop(start, start + count)
        def _(b):
            for to in range(k):
                turned[to, b] = own[b, :, to * rows : (to + 1) * rows].T

        if half == 1:
            pl.semaphore_wait(barrier, n_row * n_col - 1)
        send_own(half, 0)

    edges = [
        remote(
            ext.at[pl.ds(STEP + v * (rows - STEP), STEP)], ext.at[pl.ds((1 - v) * (rows + STEP), STEP)],
            edge_send.at[v], edge_recv.at[v], (row + 2 * v - 1, col),
        )
        for v in range(2)
    ]
    lines = [
        remote(
            strip.at[pl.ds(h * 16, 16)], halo.at[pl.ds((1 - h) * 16, 16)],
            side_send.at[h], side_recv.at[h], (row, col + 2 * h - 1),
        )
        for h in range(2)
    ]
    corners = [
        [
            remote(
                corner.at[pl.ds((2 * v + h) * 16, 16)], corner_halo.at[pl.ds((3 - 2 * v - h) * 16, 16)],
                side_send.at[2 + 2 * v + h], side_recv.at[2 + 2 * v + h], (row + 2 * v - 1, col + 2 * h - 1),
            )
            for h in range(2)
        ]
        for v in range(2)
    ]

    def swap(g):
        ext[g * BLOCK + STEP : (g + 1) * BLOCK + STEP] = jnp.transpose(feat[:, g * BLOCK : (g + 1) * BLOCK, :], (1, 0, 2))

    for load in loads:
        load.wait()
    for v in range(2):
        swap(v * (blocks - 1))
        pl.when(has_row[v])(lambda: edges[v].start())
        found = jnp.zeros((32, 2 * ch), F32)
        for s in range(2):
            y = STEP + v * (rows - STEP) + 2 * s
            found = found + lax.dot_general(picks(s, cols), ext[y : y + 2].reshape(2 * ch, cols), NT, preferred_element_type=F32)
        corner[v * 32 : (v + 1) * 32, :] = found.astype(BF16)
        for h in range(2):
            pl.when(has_row[v] & has_col[h])(lambda: corners[v][h].start())
    for g in range(1, blocks - 1):
        swap(g)
    found = jnp.zeros((32, quarter * ch), F32)
    for s in range(4):
        own_lines = ext[STEP + s * quarter : STEP + (s + 1) * quarter].reshape(quarter * ch, cols)
        found = found + lax.dot_general(picks(s, cols), own_lines, NT, preferred_element_type=F32)
    strip[...] = found.astype(BF16)
    for h in range(2):
        pl.when(has_col[h])(lambda: lines[h].start())
    for i in range(1, AHEAD):
        for half in (1, 0):
            send_own(half, i)
    tick(0)

    for load in small:
        load.wait()
    toeplitz[...] = jnp.zeros_like(toeplitz)
    for n in range(4):
        for ky in range(3):
            for kx in range(3):
                start = (n + ky) * span + kx * ch
                toeplitz[n * ch : (n + 1) * ch, start : start + ch] = w_ref[3 * ky + kx]
    wide_head = HALF * ch
    tall_head = head.shape[0]
    spread = jnp.where(lax.div(iota((tall_head, bins), 0), HALF) == iota((tall_head, bins), 1), 1.0, 0.0).astype(BF16)
    tile = jnp.where(iota((ch, wide_head), 0) == lax.rem(iota((ch, wide_head), 1), ch), 1.0, 0.0).astype(BF16)

    def same_row():
        r = lax.rem(iota((tall_head, wide_head), 0), HALF)
        place = lax.div(iota((tall_head, wide_head), 1), ch)
        return r == STEP * lax.rem(place, 2) + lax.div(place, 2)

    copies = jnp.dot(spread, wh_ref[...], preferred_element_type=F32).astype(BF16)
    copies = jnp.dot(copies, tile, preferred_element_type=F32)
    head[...] = jnp.where(same_row(), copies, 0.0).astype(BF16)
    eye = jnp.where(iota((wide_head, wide_head), 0) == iota((wide_head, wide_head), 1), 1.0, 0.0).astype(BF16)
    head_t[...] = jnp.zeros_like(head_t)
    head_t[:, 0:tall_head] = lax.dot_general(eye, head[...], NT, preferred_element_type=F32).astype(BF16)
    bias_c[...] = jnp.broadcast_to(jnp.concatenate([to_column(bc_ref[...])] * 4, axis=0), bias_c.shape)
    bias_h[...] = jnp.broadcast_to(to_column(bh_ref[...])[:, :, None], bias_h.shape)
    my_rows = valid_ref[:, pl.ds(pl.multiple_of(row * rows, rows), rows)].astype(F32)
    valid_r[...] = jnp.broadcast_to(to_column(my_rows), valid_r.shape)
    for acc in (gw_acc, gh_acc, hb_acc, cb_acc, loss_acc, dlog):
        acc[...] = jnp.zeros_like(acc)

    tick(1)

    def widen(e):
        edge = side[e].astype(F32)
        edge = jnp.concatenate([edge] * (cols // 128), axis=1)
        lane = iota((ch, cols), 1)
        line = ext[e]
        middle = line.astype(F32)
        left = jnp.where(lane < STEP, edge, pltpu.roll(middle, STEP, 1))
        right = jnp.where(lane >= cols - STEP, edge, pltpu.roll(middle, cols - STEP, 1))
        start = pl.multiple_of((lax.rem(e, STEP) * group + lax.div(e, STEP)) * span, span)
        wide[pl.ds(start, ch), :] = left.astype(BF16)
        wide[pl.ds(start + ch, ch), :] = line
        wide[pl.ds(start + 2 * ch, ch), :] = right.astype(BF16)

    def places(seg):
        r, c = iota((32, 128), 0), iota((32, 128), 1)
        at = jnp.where(r < 16, r - 4 * seg, r - 16 - 4 * seg)
        want = jnp.where(r < 16, at, at + 128 - STEP)
        return jnp.where((at >= 0) & (at < STEP) & (c == want), 1.0, 0.0).astype(BF16)

    for v in range(2):
        pl.when(has_col[v])(lambda: lines[1 - v].wait_recv())
        pl.when(has_row[v])(lambda: edges[1 - v].wait_recv())
        for h in range(2):
            pl.when(has_row[v] & has_col[h])(lambda: corners[1 - v][1 - h].wait_recv())
    for s in range(4):
        put = lax.dot_general(halo[...], places(s), TN, preferred_element_type=F32).astype(BF16)
        side[STEP + s * quarter : STEP + (s + 1) * quarter] = put.reshape(quarter, ch, 128)

    for s in range(4):
        @pl.loop(STEP + s * quarter, STEP + (s + 1) * quarter, unroll=4)
        def _(e):
            widen(e)

        if s % 2:
            tick(2 + s // 2)

    for v in range(2):
        for s in range(2):
            y = v * (rows + STEP) + 2 * s
            put = lax.dot_general(corner_halo[v * 32 : (v + 1) * 32, :], places(s), TN, preferred_element_type=F32).astype(BF16)
            side[y : y + 2] = put.reshape(2, ch, 128)
    for e in (*range(STEP), *range(rows + STEP, rows + 2 * STEP)):
        widen(jnp.int32(e))

    def window(r, i):
        start = pl.multiple_of((r * group + STEP * i) * span, span)
        return wide[pl.ds(start, tall), :]

    @pl.loop(0, blocks)
    def _(i):
        for r in range(STEP):
            pre[i, r] = jnp.dot(toeplitz[...], window(r, i), preferred_element_type=F32) + bias_c[...]

        @pl.when(lax.rem(i, 2) == 1)
        def _():
            tick(4 + lax.div(i, 2))

    for i in range(4 + blocks // 2, blocks):
        tick(i)

    lanes = cols // 128
    half_ch = 2 * ch

    @pl.loop(0, blocks)
    def _(i):
        for h in range(2):
            for r in range(STEP):
                v = pre[i, r, h * half_ch : (h + 1) * half_ch, :]
                a = jnp.where(v > 0, v, jnp.exp(jnp.minimum(v, 0.0)) - 1.0)
                act[r * half_ch : (r + 1) * half_ch, h * cols : (h + 1) * cols] = a.astype(BF16)
            logits[h] = jnp.dot(head[...], act[:, h * cols : (h + 1) * cols], preferred_element_type=F32)
        for source in range(k):
            for half in range(2):
                start, count, _ = halves[half]
                pltpu.make_async_copy(
                    turned.at[0, pl.ds(start, count), chunk(i)], mirror.at[source, pl.ds(start, count), chunk(i)],
                    mirror_recv.at[source, half, i],
                ).wait()
        for piece in range(lanes):
            at = pl.ds(piece * 128, 128)
            both = own[:, chunk(i), at].astype(F32) + mirror[piece * 128 // rows, :, chunk(i), :].astype(F32)
            mine = valid_ref[:, pl.ds(pl.multiple_of(col * cols + piece * 128, 128), 128)].astype(F32)
            for h in range(2):
                s = both[:, h * HALF : (h + 1) * HALF, :]
                et = jnp.exp((s - jnp.max(s, axis=0, keepdims=True)) * 0.5)
                es = jnp.sum(et, axis=0)
                lg = logits[h, 0 : bins * HALF, piece * 128 : (piece + 1) * 128].reshape(bins, HALF, 128) + bias_h[...]
                z = lg - jnp.max(lg, axis=0, keepdims=True)
                ez = jnp.exp(z)
                zs = jnp.sum(ez, axis=0)
                y = pl.multiple_of(i * BLOCK + h * HALF, HALF)
                weight = valid_r[pl.ds(y, HALF), :] * mine
                scale = 1.0 / es
                loss = weight * (jnp.log(zs) - jnp.sum(et * z, axis=0) * scale)
                pair_ref[pl.ds(y, HALF), at] = loss
                loss_acc[...] += loss
                fixed = weight * (1.0 / total)
                d = ez * (fixed * (1.0 / zs))[None] - et * (fixed * scale)[None]
                d = d.reshape(bins * HALF, 128).astype(BF16)
                dlog[0 : bins * HALF, h * cols + piece * 128 : h * cols + (piece + 1) * 128] = d
                hb_acc[...] += d.astype(F32)
        for h in range(2):
            back = jnp.dot(head_t[...], dlog[:, h * cols : (h + 1) * cols], preferred_element_type=F32)
            for r in range(STEP):
                v = pre[i, r, h * half_ch : (h + 1) * half_ch, :]
                slope = jnp.exp(jnp.minimum(v, 0.0))
                g = (back[r * half_ch : (r + 1) * half_ch, :] * slope).astype(BF16)
                dpre[h * half_ch : (h + 1) * half_ch, r * cols : (r + 1) * cols] = g
                g = g.astype(F32)
                cb_acc[...] += g[:ch] + g[ch:]
        gh_acc[...] += lax.dot_general(dlog[0:tall_head, :], act[...], NT, preferred_element_type=F32)
        windows = jnp.concatenate([window(r, i) for r in range(STEP)], axis=1)
        gw_acc[...] += lax.dot_general(windows, dpre[...], NT, preferred_element_type=F32)

    if height > 5 * ch:
        part_sum[5 * ch :, :] = jnp.zeros((height - 5 * ch, 2 * ch), F32)
    for ky in range(3):
        taps = functools.reduce(
            jnp.add, [gw_acc[(n + ky) * span : (n + ky + 1) * span, n * ch : (n + 1) * ch] for n in range(4)]
        )
        for kx in range(3):
            tap = 3 * ky + kx
            start = tap // 2 * ch
            part_sum[start : start + ch, tap % 2 * ch : (tap % 2 + 1) * ch] = taps[kx * ch : (kx + 1) * ch, :].T
    gh = jnp.where(same_row(), gh_acc[...], 0.0)
    gh = functools.reduce(jnp.add, [gh[:, n * ch : (n + 1) * ch] for n in range(HALF)])
    gh = jnp.sum(gh[0 : bins * HALF].reshape(bins, HALF, ch), axis=1)
    start = 4 * ch
    part_sum[start : start + ch, ch:] = jnp.zeros((ch, ch), F32)
    part_sum[start : start + bins, ch:] = gh
    hb = jnp.sum(jnp.sum(hb_acc[...].reshape(bins, HALF, 128), axis=1), axis=1, keepdims=True)
    part_sum[start + 40 : start + 41, ch : ch + bins] = to_line(hb)
    part_sum[start + 41 : start + 42, ch:] = to_line(jnp.sum(cb_acc[...], axis=1, keepdims=True))
    part_sum[start + 42 : start + 43, ch : ch + 1] = jnp.sum(jnp.sum(loss_acc[...], axis=0, keepdims=True), axis=1, keepdims=True)

    size = height // n_row

    def piece_of(index):
        return pl.ds(pl.multiple_of(index * size, 8), size)

    row_peers = [lax.rem(row + o, n_row) for o in range(1, n_row)]
    col_peers = [lax.rem(col + o, n_col) for o in range(1, n_col)]
    copies = [
        remote(part_sum.at[piece_of(peer)], row_slots.at[o], rs_send.at[o], rs_recv.at[o], (peer, col))
        for o, peer in enumerate(row_peers)
    ]
    for copy in copies:
        copy.start()
    added = part_sum[piece_of(row), :]
    for o, copy in enumerate(copies):
        copy.wait_recv()
        added = added + row_slots[o]
    part[0] = added
    col_slots[col] = added
    col_copies = [
        remote(part.at[0], col_slots.at[col], col_send.at[o], col_recv.at[o], (row, peer)) for o, peer in enumerate(col_peers)
    ]
    for copy in col_copies:
        copy.start()
    for copy in col_copies:
        copy.wait_recv()
    added = col_slots[0]
    for c in range(1, n_col):
        added = added + col_slots[c]
    part[1] = added
    sums_ref[piece_of(row), :] = added
    last = [
        remote(part.at[1], sums_ref.at[piece_of(row)], ag_send.at[o], ag_recv.at[o], (peer, col))
        for o, peer in enumerate(row_peers)
    ]
    for copy in last:
        copy.start()

    @pl.loop(0, blocks)
    def _(i):
        for half in range(2):
            sent_own(half, i)
            if bounce:
                @pl.when(straight[half])
                def _():
                    for to in range(k):
                        second_hop(half, to, i).wait_send()

    for v in range(2):
        pl.when(has_row[v])(lambda: edges[v].wait_send())
        pl.when(has_col[v])(lambda: lines[v].wait_send())
        for h in range(2):
            pl.when(has_row[v] & has_col[h])(lambda: corners[v][h].wait_send())
    for copy in copies + col_copies + last:
        copy.wait_send()
    for copy in last:
        copy.wait_recv()


def unpack_kernel(ch, bins, pair_in, sums, valid, pair_ref, loss_ref, gw_ref, cb_ref, gh_ref, hb_ref):
    pair_ref[...] = pair_in[...]
    for tap in range(9):
        start = tap // 2 * ch
        gw_ref[tap] = sums[start : start + ch, tap % 2 * ch : (tap % 2 + 1) * ch]
    start = 4 * ch
    gh_ref[...] = sums[start : start + bins, ch:]
    hb_ref[...] = sums[start + 40 : start + 41, ch : ch + bins]
    cb_ref[...] = sums[start + 41 : start + 42, ch:]
    count = jnp.sum(valid[...].astype(F32), axis=1, keepdims=True)
    loss_ref[...] = sums[start + 42 : start + 43, ch : ch + 1] / (count * count)


def on_device(teacher, features, valid, w_conv, b_conv, w_head, b_head):
    bins, rows, cols = teacher.shape
    ch = features.shape[0]
    n_row, n_col = lax.axis_size("row"), lax.axis_size("col")
    k = n_row // n_col
    blocks = rows // BLOCK
    low = bins // 2
    tall_head = -(-bins * HALF // 16) * 16
    deep_head = -(-bins * HALF // 128) * 128
    height = -(-5 * ch // (8 * n_row)) * 8 * n_row
    size = height // n_row
    quarter = rows // 4
    dma = pltpu.SemaphoreType.DMA
    vmem = pl.BlockSpec(memory_space=pltpu.VMEM)
    any_ = pl.BlockSpec(memory_space=pl.ANY)
    line = valid.reshape(1, -1)
    pair, sums = pl.pallas_call(
        functools.partial(whole_kernel, n_row, n_col, rows, cols, ch, bins, height),
        name="distil",
        out_shape=(jax.ShapeDtypeStruct((rows, cols), F32), jax.ShapeDtypeStruct((height, 2 * ch), F32)),
        in_specs=[any_] * 7,
        out_specs=(vmem, vmem),
        scratch_shapes=[
            pltpu.VMEM((bins, rows, cols), BF16),
            pltpu.VMEM((k, bins, rows, rows), BF16),
            pltpu.VMEM((k, bins, rows, rows), BF16),
            pltpu.VMEM((k, low, rows, rows), BF16),
            pltpu.VMEM((k, bins - low, rows, rows), BF16),
            pltpu.VMEM((ch, rows, cols), BF16),
            pltpu.VMEM((rows + 2 * STEP, ch, cols), BF16),
            pltpu.VMEM((32, quarter * ch), BF16),
            pltpu.VMEM((32, quarter * ch), BF16),
            pltpu.VMEM((64, 2 * ch), BF16),
            pltpu.VMEM((64, 2 * ch), BF16),
            pltpu.VMEM((rows + 2 * STEP, ch, 128), BF16),
            pltpu.VMEM(((rows + 2 * STEP) * 3 * ch, cols), BF16),
            pltpu.VMEM((blocks, STEP, 4 * ch, cols), F32),
            pltpu.VMEM((4 * ch, 18 * ch), BF16),
            pltpu.VMEM((tall_head, HALF * ch), BF16),
            pltpu.VMEM((HALF * ch, deep_head), BF16),
            pltpu.VMEM((4 * ch, cols), F32),
            pltpu.VMEM((bins, HALF, 128), F32),
            pltpu.VMEM((rows, 128), F32),
            pltpu.VMEM((HALF * ch, 2 * cols), BF16),
            pltpu.VMEM((2, tall_head, cols), F32),
            pltpu.VMEM((deep_head, 2 * cols), BF16),
            pltpu.VMEM((4 * ch, STEP * cols), BF16),
            pltpu.VMEM((18 * ch, 4 * ch), F32),
            pltpu.VMEM((tall_head, HALF * ch), F32),
            pltpu.VMEM((bins * HALF, 128), F32),
            pltpu.VMEM((ch, cols), F32),
            pltpu.VMEM((HALF, 128), F32),
            pltpu.VMEM((height, 2 * ch), F32),
            pltpu.VMEM((n_row - 1, size, 2 * ch), F32),
            pltpu.VMEM((2, size, 2 * ch), F32),
            pltpu.VMEM((n_col, size, 2 * ch), F32),
            pltpu.VMEM(line.shape, jnp.int32),
            pltpu.VMEM((9, ch, ch), BF16),
            pltpu.VMEM((1, ch), F32),
            pltpu.VMEM((bins, ch), BF16),
            pltpu.VMEM((1, bins), F32),
            dma((5,)),
            dma((6,)), dma((2, k, blocks)), dma((k, 2, blocks)), dma((2, blocks)), dma((2, k, blocks)),
            dma((2,)), dma((2,)), dma((6,)), dma((6,)),
            dma((n_row - 1,)), dma((n_row - 1,)), dma((n_col - 1,)), dma((n_col - 1,)), dma((n_row - 1,)), dma((n_row - 1,)),
        ],
        compiler_params=pltpu.CompilerParams(collective_id=0, has_side_effects=True, vmem_limit_bytes=VMEM_BYTES),
    )(
        teacher, features, line, jnp.transpose(w_conv, (2, 3, 0, 1)).reshape(9, ch, ch),
        b_conv.reshape(1, ch), w_head, b_head.reshape(1, bins),
    )
    pair, loss, gw, cb, gh, hb = pl.pallas_call(
        functools.partial(unpack_kernel, ch, bins),
        name="unpack",
        out_shape=(
            jax.ShapeDtypeStruct((rows, cols), F32),
            jax.ShapeDtypeStruct((1, 1), F32),
            jax.ShapeDtypeStruct((9, ch, ch), F32),
            jax.ShapeDtypeStruct((1, ch), F32),
            jax.ShapeDtypeStruct((bins, ch), F32),
            jax.ShapeDtypeStruct((1, bins), F32),
        ),
        in_specs=[vmem] * 3,
        out_specs=(vmem,) * 6,
    )(pair, sums, line)
    gw = jnp.transpose(gw.reshape(3, 3, ch, ch), (2, 3, 0, 1))
    return pair, loss.reshape(()), gw, cb.reshape(ch), gh, hb.reshape(bins)


def solution(mesh):
    in_specs = (P(None, "row", "col"), P(None, "row", "col"), P(), P(), P(), P(), P())
    out_specs = (P("row", "col"), P(), P(), P(), P(), P())
    return jax.shard_map(
        on_device, mesh=mesh, in_specs=in_specs, out_specs=out_specs, check_vma=False
    )
```

```python
import functools

import jax
import jax.numpy as jnp
from jax import lax
from jax.experimental import pallas as pl
from jax.experimental.pallas import tpu as pltpu
from jax.sharding import PartitionSpec as P

STEP = 4
BLOCK = 16
HALF = 8
AHEAD = 2
VMEM_BYTES = 60 * 1024 * 1024
MESH = pl.DeviceIdType.MESH
BF16, F32 = jnp.bfloat16, jnp.float32
NT = (((1,), (1,)), ((), ()))
TN = (((0,), (0,)), ((), ()))


def iota(shape, dim):
    return lax.broadcasted_iota(jnp.int32, shape, dim)


def to_column(line):
    n = line.shape[1]
    return jnp.sum(jnp.where(iota((n, n), 0) == iota((n, n), 1), jnp.broadcast_to(line, (n, n)), 0.0), axis=1, keepdims=True)


def to_line(column):
    n = column.shape[0]
    return jnp.sum(jnp.where(iota((n, n), 0) == iota((n, n), 1), jnp.broadcast_to(column, (n, n)), 0.0), axis=0, keepdims=True)


def picks(seg, cols):
    r, c = iota((32, cols), 0), iota((32, cols), 1)
    at = jnp.where(r < 16, r - 4 * seg, r - 16 - 4 * seg)
    want = jnp.where(r < 16, at, at + cols - STEP)
    return jnp.where((at >= 0) & (at < STEP) & (c == want), 1.0, 0.0).astype(BF16)


def whole_kernel(
    n_row, n_col, rows, cols, ch, bins, height,
    teacher_hbm, feat_hbm, *rest,
):
    small_hbm, rest = rest[:5], rest[5:]
    (
        pair_ref, sums_ref,
        own, turned, mirror, hop_x, hop_y, feat, ext, strip, halo, corner, corner_halo, side, wide, pre,
        toeplitz, head, head_t, bias_c, bias_h, valid_r,
        act, logits, dlog, dpre, gw_acc, gh_acc, hb_acc, cb_acc, loss_acc,
        part_sum, row_slots, part, col_slots,
        valid_ref, w_ref, bc_ref, wh_ref, bh_ref, small_sem,
        load_sem, own_send, mirror_recv, hop_recv, fwd_send, edge_send, edge_recv, side_send, side_recv,
        rs_send, rs_recv, col_send, col_recv, ag_send, ag_recv,
    ) = rest
    k = n_row // n_col
    bounce = n_col == 4 and k == 2
    blocks = rows // BLOCK
    group = (rows + 2 * STEP) // STEP
    span = 3 * ch
    tall = 6 * span
    total = rows * n_row
    low = bins // 2
    halves = ((0, low, hop_x), (low, bins - low, hop_y))
    row, col = lax.axis_index("row"), lax.axis_index("col")
    p, u = lax.div(row, k), lax.rem(row, k)
    at_home = p == col
    if bounce:
        p_y, p_x, z_y, z_x = lax.div(p, 2), lax.rem(p, 2), lax.div(col, 2), lax.rem(col, 2)
        near = (p + 1 - 2 * p_x, p + 2 - 4 * p_y)
        straight = (p_x == z_x, p_y == z_y)

    barrier = pltpu.get_barrier_semaphore()

    @pl.loop(1, n_row * n_col)
    def _(o):
        peer = lax.rem(row * n_col + col + o, n_row * n_col)
        pl.semaphore_signal(
            barrier, inc=1, device_id=(lax.div(peer, n_col), lax.rem(peer, n_col)), device_id_type=MESH
        )

    quarter = rows // 4
    loads = [
        pltpu.make_async_copy(feat_hbm.at[:, pl.ds(s * quarter, quarter)], feat.at[:, pl.ds(s * quarter, quarter)], load_sem.at[s])
        for s in range(4)
    ]
    load_own = [
        pltpu.make_async_copy(teacher_hbm.at[pl.ds(start, count)], own.at[pl.ds(start, count)], load_sem.at[4 + half])
        for half, (start, count, _) in enumerate(halves)
    ]
    load_own[1].start()
    load_own[0].start()
    for load in loads:
        load.start()
    small = [
        pltpu.make_async_copy(src, dst, small_sem.at[n])
        for n, (src, dst) in enumerate(zip(small_hbm, (valid_ref, w_ref, bc_ref, wh_ref, bh_ref)))
    ]
    for load in small:
        load.start()

    def remote(src, dst, send_sem, recv_sem, device):
        return pltpu.make_async_remote_copy(
            src_ref=src, dst_ref=dst, send_sem=send_sem, recv_sem=recv_sem, device_id=device, device_id_type=MESH
        )

    def chunk(i):
        return pl.ds(pl.multiple_of(i * BLOCK, BLOCK), BLOCK)

    def direct(half, to, i):
        start, count, _ = halves[half]
        return remote(
            turned.at[to, pl.ds(start, count), chunk(i)], mirror.at[u, pl.ds(start, count), chunk(i)],
            own_send.at[half, to, i], mirror_recv.at[u, half, i], (col * k + to, p),
        )

    def stay(half, to, i):
        start, count, _ = halves[half]
        return pltpu.make_async_copy(
            turned.at[to, pl.ds(start, count), chunk(i)], mirror.at[u, pl.ds(start, count), chunk(i)],
            mirror_recv.at[u, half, i],
        )

    def first_hop(half, i):
        start, count, hop = halves[half]
        return remote(
            turned.at[:, pl.ds(start, count), chunk(i)], hop.at[:, :, chunk(i)],
            own_send.at[half, 0, i], hop_recv.at[half, i], (near[half] * k + u, col),
        )

    def second_hop(half, to, i):
        start, count, hop = halves[half]
        return remote(
            hop.at[to, :, chunk(i)], mirror.at[u, pl.ds(start, count), chunk(i)],
            fwd_send.at[half, to, i], mirror_recv.at[u, half, i], (col * k + to, near[half]),
        )

    def send_own(half, i):
        def go_direct():
            for to in range(k):
                here = at_home & (u == to)

                @pl.when(here)
                def _():
                    stay(half, to, i).start()

                @pl.when(jnp.logical_not(here))
                def _():
                    direct(half, to, i).start()

        if bounce:
            pl.when(straight[half])(go_direct)
            pl.when(jnp.logical_not(straight[half]))(lambda: first_hop(half, i).start())
        else:
            go_direct()

    def sent_own(half, i):
        def went_direct():
            for to in range(k):
                @pl.when(jnp.logical_not(at_home & (u == to)))
                def _():
                    direct(half, to, i).wait_send()

        if bounce:
            pl.when(straight[half])(went_direct)
            pl.when(jnp.logical_not(straight[half]))(lambda: first_hop(half, i).wait_send())
        else:
            went_direct()

    def tick(i):
        if bounce:
            for half in (1, 0):
                @pl.when(straight[half])
                def _():
                    first_hop(half, i).wait_recv()
                    for to in range(k):
                        second_hop(half, to, i).start()

        @pl.when(i + AHEAD < blocks)
        def _():
            for half in (1, 0):
                send_own(half, i + AHEAD)

    has_up, has_down, has_left, has_right = row > 0, row < n_row - 1, col > 0, col < n_col - 1
    has_row, has_col = (has_up, has_down), (has_left, has_right)

    for v in range(2):
        @pl.when(jnp.logical_not(has_row[v]))
        def _():
            ext[v * (rows + STEP) : v * (rows + STEP) + STEP] = jnp.zeros((STEP, ch, cols), BF16)

        @pl.when(jnp.logical_not(has_col[v]))
        def _():
            halo[v * 16 : (v + 1) * 16, :] = jnp.zeros((16, quarter * ch), BF16)

        for h in range(2):
            @pl.when(jnp.logical_not(has_row[v] & has_col[h]))
            def _():
                corner_halo[(2 * v + h) * 16 : (2 * v + h + 1) * 16, :] = jnp.zeros((16, 2 * ch), BF16)

    for half in (1, 0):
        start, count, _ = halves[half]
        load_own[half].wait()

        @pl.loop(start, start + count)
        def _(b):
            for to in range(k):
                turned[to, b] = own[b, :, to * rows : (to + 1) * rows].T

        if half == 1:
            pl.semaphore_wait(barrier, n_row * n_col - 1)
        send_own(half, 0)

    edges = [
        remote(
            ext.at[pl.ds(STEP + v * (rows - STEP), STEP)], ext.at[pl.ds((1 - v) * (rows + STEP), STEP)],
            edge_send.at[v], edge_recv.at[v], (row + 2 * v - 1, col),
        )
        for v in range(2)
    ]
    lines = [
        remote(
            strip.at[pl.ds(h * 16, 16)], halo.at[pl.ds((1 - h) * 16, 16)],
            side_send.at[h], side_recv.at[h], (row, col + 2 * h - 1),
        )
        for h in range(2)
    ]
    corners = [
        [
            remote(
                corner.at[pl.ds((2 * v + h) * 16, 16)], corner_halo.at[pl.ds((3 - 2 * v - h) * 16, 16)],
                side_send.at[2 + 2 * v + h], side_recv.at[2 + 2 * v + h], (row + 2 * v - 1, col + 2 * h - 1),
            )
            for h in range(2)
        ]
        for v in range(2)
    ]

    def swap(g):
        ext[g * BLOCK + STEP : (g + 1) * BLOCK + STEP] = jnp.transpose(feat[:, g * BLOCK : (g + 1) * BLOCK, :], (1, 0, 2))

    for load in loads:
        load.wait()
    for v in range(2):
        swap(v * (blocks - 1))
        pl.when(has_row[v])(lambda: edges[v].start())
        found = jnp.zeros((32, 2 * ch), F32)
        for s in range(2):
            y = STEP + v * (rows - STEP) + 2 * s
            found = found + lax.dot_general(picks(s, cols), ext[y : y + 2].reshape(2 * ch, cols), NT, preferred_element_type=F32)
        corner[v * 32 : (v + 1) * 32, :] = found.astype(BF16)
        for h in range(2):
            pl.when(has_row[v] & has_col[h])(lambda: corners[v][h].start())
    for g in range(1, blocks - 1):
        swap(g)
    found = jnp.zeros((32, quarter * ch), F32)
    for s in range(4):
        own_lines = ext[STEP + s * quarter : STEP + (s + 1) * quarter].reshape(quarter * ch, cols)
        found = found + lax.dot_general(picks(s, cols), own_lines, NT, preferred_element_type=F32)
    strip[...] = found.astype(BF16)
    for h in range(2):
        pl.when(has_col[h])(lambda: lines[h].start())
    for i in range(1, AHEAD):
        for half in (1, 0):
            send_own(half, i)
    tick(0)

    for load in small:
        load.wait()
    toeplitz[...] = jnp.zeros_like(toeplitz)
    for n in range(4):
        for ky in range(3):
            for kx in range(3):
                start = (n + ky) * span + kx * ch
                toeplitz[n * ch : (n + 1) * ch, start : start + ch] = w_ref[3 * ky + kx]
    wide_head = HALF * ch
    tall_head = head.shape[0]
    spread = jnp.where(lax.div(iota((tall_head, bins), 0), HALF) == iota((tall_head, bins), 1), 1.0, 0.0).astype(BF16)
    tile = jnp.where(iota((ch, wide_head), 0) == lax.rem(iota((ch, wide_head), 1), ch), 1.0, 0.0).astype(BF16)

    def same_row():
        r = lax.rem(iota((tall_head, wide_head), 0), HALF)
        place = lax.div(iota((tall_head, wide_head), 1), ch)
        return r == STEP * lax.rem(place, 2) + lax.div(place, 2)

    copies = jnp.dot(spread, wh_ref[...], preferred_element_type=F32).astype(BF16)
    copies = jnp.dot(copies, tile, preferred_element_type=F32)
    head[...] = jnp.where(same_row(), copies, 0.0).astype(BF16)
    eye = jnp.where(iota((wide_head, wide_head), 0) == iota((wide_head, wide_head), 1), 1.0, 0.0).astype(BF16)
    head_t[...] = jnp.zeros_like(head_t)
    head_t[:, 0:tall_head] = lax.dot_general(eye, head[...], NT, preferred_element_type=F32).astype(BF16)
    bias_c[...] = jnp.broadcast_to(jnp.concatenate([to_column(bc_ref[...])] * 4, axis=0), bias_c.shape)
    bias_h[...] = jnp.broadcast_to(to_column(bh_ref[...])[:, :, None], bias_h.shape)
    my_rows = valid_ref[:, pl.ds(pl.multiple_of(row * rows, rows), rows)].astype(F32)
    valid_r[...] = jnp.broadcast_to(to_column(my_rows), valid_r.shape)
    for acc in (gw_acc, gh_acc, hb_acc, cb_acc, loss_acc, dlog):
        acc[...] = jnp.zeros_like(acc)

    tick(1)

    def widen(e):
        edge = side[e].astype(F32)
        edge = jnp.concatenate([edge] * (cols // 128), axis=1)
        lane = iota((ch, cols), 1)
        line = ext[e]
        middle = line.astype(F32)
        left = jnp.where(lane < STEP, edge, pltpu.roll(middle, STEP, 1))
        right = jnp.where(lane >= cols - STEP, edge, pltpu.roll(middle, cols - STEP, 1))
        start = pl.multiple_of((lax.rem(e, STEP) * group + lax.div(e, STEP)) * span, span)
        wide[pl.ds(start, ch), :] = left.astype(BF16)
        wide[pl.ds(start + ch, ch), :] = line
        wide[pl.ds(start + 2 * ch, ch), :] = right.astype(BF16)

    def places(seg):
        r, c = iota((32, 128), 0), iota((32, 128), 1)
        at = jnp.where(r < 16, r - 4 * seg, r - 16 - 4 * seg)
        want = jnp.where(r < 16, at, at + 128 - STEP)
        return jnp.where((at >= 0) & (at < STEP) & (c == want), 1.0, 0.0).astype(BF16)

    for v in range(2):
        pl.when(has_col[v])(lambda: lines[1 - v].wait_recv())
        pl.when(has_row[v])(lambda: edges[1 - v].wait_recv())
        for h in range(2):
            pl.when(has_row[v] & has_col[h])(lambda: corners[1 - v][1 - h].wait_recv())
    for s in range(4):
        put = lax.dot_general(halo[...], places(s), TN, preferred_element_type=F32).astype(BF16)
        side[STEP + s * quarter : STEP + (s + 1) * quarter] = put.reshape(quarter, ch, 128)

    for s in range(4):
        @pl.loop(STEP + s * quarter, STEP + (s + 1) * quarter, unroll=4)
        def _(e):
            widen(e)

        if s % 2:
            tick(2 + s // 2)

    for v in range(2):
        for s in range(2):
            y = v * (rows + STEP) + 2 * s
            put = lax.dot_general(corner_halo[v * 32 : (v + 1) * 32, :], places(s), TN, preferred_element_type=F32).astype(BF16)
            side[y : y + 2] = put.reshape(2, ch, 128)
    for e in (*range(STEP), *range(rows + STEP, rows + 2 * STEP)):
        widen(jnp.int32(e))

    def window(r, i):
        start = pl.multiple_of((r * group + STEP * i) * span, span)
        return wide[pl.ds(start, tall), :]

    @pl.loop(0, blocks)
    def _(i):
        for r in range(STEP):
            pre[i, r] = jnp.dot(toeplitz[...], window(r, i), preferred_element_type=F32) + bias_c[...]

        @pl.when(i < blocks - 4)
        def _():
            tick(4 + i)

    lanes = cols // 128
    half_ch = 2 * ch

    @pl.loop(0, blocks)
    def _(i):
        for h in range(2):
            for r in range(STEP):
                v = pre[i, r, h * half_ch : (h + 1) * half_ch, :]
                a = jnp.where(v > 0, v, jnp.exp(jnp.minimum(v, 0.0)) - 1.0)
                act[r * half_ch : (r + 1) * half_ch, h * cols : (h + 1) * cols] = a.astype(BF16)
            logits[h] = jnp.dot(head[...], act[:, h * cols : (h + 1) * cols], preferred_element_type=F32)
        for piece in range(lanes):
            source = piece * 128 // rows
            for half in range(2):
                start, count, _ = halves[half]
                pltpu.make_async_copy(
                    turned.at[0, pl.ds(start, count), chunk(i)], mirror.at[source, pl.ds(start, count), chunk(i)],
                    mirror_recv.at[source, half, i],
                ).wait()
            at = pl.ds(piece * 128, 128)
            both = own[:, chunk(i), at].astype(F32) + mirror[piece * 128 // rows, :, chunk(i), :].astype(F32)
            mine = valid_ref[:, pl.ds(pl.multiple_of(col * cols + piece * 128, 128), 128)].astype(F32)
            for h in range(2):
                s = both[:, h * HALF : (h + 1) * HALF, :]
                et = jnp.exp((s - jnp.max(s, axis=0, keepdims=True)) * 0.5)
                es = jnp.sum(et, axis=0)
                lg = logits[h, 0 : bins * HALF, piece * 128 : (piece + 1) * 128].reshape(bins, HALF, 128) + bias_h[...]
                z = lg - jnp.max(lg, axis=0, keepdims=True)
                ez = jnp.exp(z)
                zs = jnp.sum(ez, axis=0)
                y = pl.multiple_of(i * BLOCK + h * HALF, HALF)
                weight = valid_r[pl.ds(y, HALF), :] * mine
                scale = 1.0 / es
                loss = weight * (jnp.log(zs) - jnp.sum(et * z, axis=0) * scale)
                pair_ref[pl.ds(y, HALF), at] = loss
                loss_acc[...] += loss
                fixed = weight * (1.0 / total)
                d = ez * (fixed * (1.0 / zs))[None] - et * (fixed * scale)[None]
                d = d.reshape(bins * HALF, 128).astype(BF16)
                dlog[0 : bins * HALF, h * cols + piece * 128 : h * cols + (piece + 1) * 128] = d
                hb_acc[...] += d.astype(F32)
        for h in range(2):
            back = jnp.dot(head_t[...], dlog[:, h * cols : (h + 1) * cols], preferred_element_type=F32)
            for r in range(STEP):
                v = pre[i, r, h * half_ch : (h + 1) * half_ch, :]
                slope = jnp.exp(jnp.minimum(v, 0.0))
                g = (back[r * half_ch : (r + 1) * half_ch, :] * slope).astype(BF16)
                dpre[h * half_ch : (h + 1) * half_ch, r * cols : (r + 1) * cols] = g
                g = g.astype(F32)
                cb_acc[...] += g[:ch] + g[ch:]
        gh_acc[...] += lax.dot_general(dlog[0:tall_head, :], act[...], NT, preferred_element_type=F32)
        windows = jnp.concatenate([window(r, i) for r in range(STEP)], axis=1)
        gw_acc[...] += lax.dot_general(windows, dpre[...], NT, preferred_element_type=F32)

    if height > 5 * ch:
        part_sum[5 * ch :, :] = jnp.zeros((height - 5 * ch, 2 * ch), F32)
    for ky in range(3):
        taps = functools.reduce(
            jnp.add, [gw_acc[(n + ky) * span : (n + ky + 1) * span, n * ch : (n + 1) * ch] for n in range(4)]
        )
        for kx in range(3):
            tap = 3 * ky + kx
            start = tap // 2 * ch
            part_sum[start : start + ch, tap % 2 * ch : (tap % 2 + 1) * ch] = taps[kx * ch : (kx + 1) * ch, :].T
    gh = jnp.where(same_row(), gh_acc[...], 0.0)
    gh = functools.reduce(jnp.add, [gh[:, n * ch : (n + 1) * ch] for n in range(HALF)])
    gh = jnp.sum(gh[0 : bins * HALF].reshape(bins, HALF, ch), axis=1)
    start = 4 * ch
    part_sum[start : start + ch, ch:] = jnp.zeros((ch, ch), F32)
    part_sum[start : start + bins, ch:] = gh
    hb = jnp.sum(jnp.sum(hb_acc[...].reshape(bins, HALF, 128), axis=1), axis=1, keepdims=True)
    part_sum[start + 40 : start + 41, ch : ch + bins] = to_line(hb)
    part_sum[start + 41 : start + 42, ch:] = to_line(jnp.sum(cb_acc[...], axis=1, keepdims=True))
    part_sum[start + 42 : start + 43, ch : ch + 1] = jnp.sum(jnp.sum(loss_acc[...], axis=0, keepdims=True), axis=1, keepdims=True)

    size = height // n_row

    def piece_of(index):
        return pl.ds(pl.multiple_of(index * size, 8), size)

    row_peers = [lax.rem(row + o, n_row) for o in range(1, n_row)]
    col_peers = [lax.rem(col + o, n_col) for o in range(1, n_col)]
    copies = [
        remote(part_sum.at[piece_of(peer)], row_slots.at[o], rs_send.at[o], rs_recv.at[o], (peer, col))
        for o, peer in enumerate(row_peers)
    ]
    for copy in copies:
        copy.start()
    added = part_sum[piece_of(row), :]
    for o, copy in enumerate(copies):
        copy.wait_recv()
        added = added + row_slots[o]
    part[0] = added
    col_slots[col] = added
    col_copies = [
        remote(part.at[0], col_slots.at[col], col_send.at[o], col_recv.at[o], (row, peer)) for o, peer in enumerate(col_peers)
    ]
    for copy in col_copies:
        copy.start()
    for copy in col_copies:
        copy.wait_recv()
    added = col_slots[0]
    for c in range(1, n_col):
        added = added + col_slots[c]
    part[1] = added
    sums_ref[piece_of(row), :] = added
    last = [
        remote(part.at[1], sums_ref.at[piece_of(row)], ag_send.at[o], ag_recv.at[o], (peer, col))
        for o, peer in enumerate(row_peers)
    ]
    for copy in last:
        copy.start()

    @pl.loop(0, blocks)
    def _(i):
        for half in range(2):
            sent_own(half, i)
            if bounce:
                @pl.when(straight[half])
                def _():
                    for to in range(k):
                        second_hop(half, to, i).wait_send()

    for v in range(2):
        pl.when(has_row[v])(lambda: edges[v].wait_send())
        pl.when(has_col[v])(lambda: lines[v].wait_send())
        for h in range(2):
            pl.when(has_row[v] & has_col[h])(lambda: corners[v][h].wait_send())
    for copy in copies + col_copies + last:
        copy.wait_send()
    for copy in last:
        copy.wait_recv()


def unpack_kernel(ch, bins, pair_in, sums, valid, pair_ref, loss_ref, gw_ref, cb_ref, gh_ref, hb_ref):
    pair_ref[...] = pair_in[...]
    for tap in range(9):
        start = tap // 2 * ch
        gw_ref[tap] = sums[start : start + ch, tap % 2 * ch : (tap % 2 + 1) * ch]
    start = 4 * ch
    gh_ref[...] = sums[start : start + bins, ch:]
    hb_ref[...] = sums[start + 40 : start + 41, ch : ch + bins]
    cb_ref[...] = sums[start + 41 : start + 42, ch:]
    count = jnp.sum(valid[...].astype(F32), axis=1, keepdims=True)
    loss_ref[...] = sums[start + 42 : start + 43, ch : ch + 1] / (count * count)


def on_device(teacher, features, valid, w_conv, b_conv, w_head, b_head):
    bins, rows, cols = teacher.shape
    ch = features.shape[0]
    n_row, n_col = lax.axis_size("row"), lax.axis_size("col")
    k = n_row // n_col
    blocks = rows // BLOCK
    low = bins // 2
    tall_head = -(-bins * HALF // 16) * 16
    deep_head = -(-bins * HALF // 128) * 128
    height = -(-5 * ch // (8 * n_row)) * 8 * n_row
    size = height // n_row
    quarter = rows // 4
    dma = pltpu.SemaphoreType.DMA
    vmem = pl.BlockSpec(memory_space=pltpu.VMEM)
    any_ = pl.BlockSpec(memory_space=pl.ANY)
    line = valid.reshape(1, -1)
    pair, sums = pl.pallas_call(
        functools.partial(whole_kernel, n_row, n_col, rows, cols, ch, bins, height),
        name="distil",
        out_shape=(jax.ShapeDtypeStruct((rows, cols), F32), jax.ShapeDtypeStruct((height, 2 * ch), F32)),
        in_specs=[any_] * 7,
        out_specs=(vmem, vmem),
        scratch_shapes=[
            pltpu.VMEM((bins, rows, cols), BF16),
            pltpu.VMEM((k, bins, rows, rows), BF16),
            pltpu.VMEM((k, bins, rows, rows), BF16),
            pltpu.VMEM((k, low, rows, rows), BF16),
            pltpu.VMEM((k, bins - low, rows, rows), BF16),
            pltpu.VMEM((ch, rows, cols), BF16),
            pltpu.VMEM((rows + 2 * STEP, ch, cols), BF16),
            pltpu.VMEM((32, quarter * ch), BF16),
            pltpu.VMEM((32, quarter * ch), BF16),
            pltpu.VMEM((64, 2 * ch), BF16),
            pltpu.VMEM((64, 2 * ch), BF16),
            pltpu.VMEM((rows + 2 * STEP, ch, 128), BF16),
            pltpu.VMEM(((rows + 2 * STEP) * 3 * ch, cols), BF16),
            pltpu.VMEM((blocks, STEP, 4 * ch, cols), F32),
            pltpu.VMEM((4 * ch, 18 * ch), BF16),
            pltpu.VMEM((tall_head, HALF * ch), BF16),
            pltpu.VMEM((HALF * ch, deep_head), BF16),
            pltpu.VMEM((4 * ch, cols), F32),
            pltpu.VMEM((bins, HALF, 128), F32),
            pltpu.VMEM((rows, 128), F32),
            pltpu.VMEM((HALF * ch, 2 * cols), BF16),
            pltpu.VMEM((2, tall_head, cols), F32),
            pltpu.VMEM((deep_head, 2 * cols), BF16),
            pltpu.VMEM((4 * ch, STEP * cols), BF16),
            pltpu.VMEM((18 * ch, 4 * ch), F32),
            pltpu.VMEM((tall_head, HALF * ch), F32),
            pltpu.VMEM((bins * HALF, 128), F32),
            pltpu.VMEM((ch, cols), F32),
            pltpu.VMEM((HALF, 128), F32),
            pltpu.VMEM((height, 2 * ch), F32),
            pltpu.VMEM((n_row - 1, size, 2 * ch), F32),
            pltpu.VMEM((2, size, 2 * ch), F32),
            pltpu.VMEM((n_col, size, 2 * ch), F32),
            pltpu.VMEM(line.shape, jnp.int32),
            pltpu.VMEM((9, ch, ch), BF16),
            pltpu.VMEM((1, ch), F32),
            pltpu.VMEM((bins, ch), BF16),
            pltpu.VMEM((1, bins), F32),
            dma((5,)),
            dma((6,)), dma((2, k, blocks)), dma((k, 2, blocks)), dma((2, blocks)), dma((2, k, blocks)),
            dma((2,)), dma((2,)), dma((6,)), dma((6,)),
            dma((n_row - 1,)), dma((n_row - 1,)), dma((n_col - 1,)), dma((n_col - 1,)), dma((n_row - 1,)), dma((n_row - 1,)),
        ],
        compiler_params=pltpu.CompilerParams(collective_id=0, has_side_effects=True, vmem_limit_bytes=VMEM_BYTES),
    )(
        teacher, features, line, jnp.transpose(w_conv, (2, 3, 0, 1)).reshape(9, ch, ch),
        b_conv.reshape(1, ch), w_head, b_head.reshape(1, bins),
    )
    pair, loss, gw, cb, gh, hb = pl.pallas_call(
        functools.partial(unpack_kernel, ch, bins),
        name="unpack",
        out_shape=(
            jax.ShapeDtypeStruct((rows, cols), F32),
            jax.ShapeDtypeStruct((1, 1), F32),
            jax.ShapeDtypeStruct((9, ch, ch), F32),
            jax.ShapeDtypeStruct((1, ch), F32),
            jax.ShapeDtypeStruct((bins, ch), F32),
            jax.ShapeDtypeStruct((1, bins), F32),
        ),
        in_specs=[vmem] * 3,
        out_specs=(vmem,) * 6,
    )(pair, sums, line)
    gw = jnp.transpose(gw.reshape(3, 3, ch, ch), (2, 3, 0, 1))
    return pair, loss.reshape(()), gw, cb.reshape(ch), gh, hb.reshape(bins)


def solution(mesh):
    in_specs = (P(None, "row", "col"), P(None, "row", "col"), P(), P(), P(), P(), P())
    out_specs = (P("row", "col"), P(), P(), P(), P(), P())
    return jax.shard_map(
        on_device, mesh=mesh, in_specs=in_specs, out_specs=out_specs, check_vma=False
    )
```
